512 devices in a mesh: slab: 128 (over z_hi, x, y, core), cell: 4 (over z_lo).
Axes of the slice: x: 4, y: 4, z: 16 (z_hi: 4, z_lo: 4; z = z_hi * 4 + z_lo), core: 2. Of those that a mesh axis runs over, the one named last changes fastest.
Arguments:
- charges: float32 [8, 128, 2048], P(None, 'slab', 'cell'), may hold values from -6 to 6
- counts: int32 [128, 2048], P('slab', 'cell'), may hold values from 1 to 8
- projection: float32 [8, 64, 128, 2048], P(None, None, 'slab', 'cell'), may hold values from -1.2 to 1.2
- near_blocks: float32 [6, 8, 8, 128, 2048], P(None, None, None, 'slab', 'cell'), may hold values from -0.9 to 0.9
- neighbours: int32 [6, 128, 2048], P(None, 'slab', 'cell'), may hold values from 0 to 26, as said below
- spectrum: float32 [512, 64, 512], P(None, None, 'slab'), may hold values from 0.25 to 4, as said below
Outputs:
- potentials: float32 [8, 128, 2048], P(None, 'slab', 'cell')
The draws below stay inside these ranges and needn't reach their ends.
Inputs may be any that keep to these rules, and one draw needn't show every extreme that they name: `counts`: 8 is reached. neighbours[k, x, c] codes an offset in the 3 x 3 x 3 block of cells around c as in the near_field step; entry k = 0 is 13, the cell itself, and the 6 entries of a cell are distinct. spectrum[kx, kz, ky] = spectrum[(-kx) mod 512, (-kz) mod 64, (-ky) mod 512].
All inputs are finite; a program needn't handle non-finite values.
Results may differ from the reference program's by a relative error of at most 0.00005.
Values sent between devices are 32-bit elements; how exact they have to be, the bound alone decides.
A program may use at most 64 MiB of HBM per device.

```python
import jax
import jax.numpy as jnp
from jax import lax

NX = 512
NY = 512
NZ = 64
TX = 4
TY = 4
TZ = 4
PMAX = 8
NEAR = 6
NXC = 128
NYC = 128
NZC = 16
NCELL = 2048


def draw_neighbours(key, part):
    scores = jax.random.randint(key, (NXC, NCELL, 27), 0, 1 << 20)
    cand_index = lax.broadcasted_iota(jnp.int32, (NXC, NCELL, 27), 2)
    scores = jnp.where(cand_index == 13, 1 << 26, scores * 32 + cand_index)
    picked_ids = lax.top_k(scores, NEAR)[1].astype(jnp.int32)
    return jnp.transpose(picked_ids, (2, 0, 1)).astype(jnp.int32)


def draw_spectrum(key, part):
    base = jnp.exp(jax.random.uniform(key, (NX, NZ, NY), jnp.float32, jnp.log(0.25), jnp.log(4.0)))
    mirrored = jnp.roll(jnp.flip(base, (0, 1, 2)), 1, axis=(0, 1, 2))
    return ((base + mirrored) * 0.5).astype(jnp.float32)


def place_ends(entries, key, low, high):
    spot = [jax.random.randint(jax.random.fold_in(key, axis), (), 0, length) for axis, length in enumerate(entries.shape)]
    main_axis = entries.shape.index(max(entries.shape))
    neighbour = spot[:main_axis] + [(spot[main_axis] + 1) % entries.shape[main_axis]] + spot[main_axis + 1:]
    return entries.at[tuple(spot)].set(low).at[tuple(neighbour)].set(high)


def steps_of(key, dims, shards, least, high):
    level = 1.0
    for dim, blocks in shards:
        steps = jax.random.uniform(jax.random.fold_in(jax.random.fold_in(key, 6), dim), (blocks,), jnp.float32, least / len(shards), high / len(shards))
        level = level * jnp.repeat(jnp.exp(steps), dims[dim] // blocks).reshape((-1,) + (1,) * (len(dims) - 1 - dim))
    return level


def scatter_about(own_key, shape, scale, limit, pieces=(), held_as=jnp.bfloat16):
    drawn = jax.random.normal(own_key, shape, jnp.float32) * scale
    if len(pieces) > 0:
        drawn = steps_of(own_key, shape, pieces, -0.22, 0.18) * drawn
    return jnp.clip(drawn, min=-limit, max=limit).astype(held_as)


def setup_inputs(seed: int = 0) -> dict:
    arg_keys = jax.random.split(jax.random.key(seed), 7)
    return {
        "charges": scatter_about(arg_keys[0], (PMAX, NXC, NCELL), 1.0, 6.0, ((1, 128), (2, 4)), jnp.float32),
        "counts": place_ends(jax.random.randint(arg_keys[1], (NXC, NCELL), 1, PMAX + 1), jax.random.fold_in(arg_keys[1], 1), 1, PMAX).astype(jnp.int32),
        "projection": scatter_about(arg_keys[2], (PMAX, TX * TY * TZ, NXC, NCELL), 0.2, 1.2, ((2, 128), (3, 4)), jnp.float32),
        "near_blocks": scatter_about(arg_keys[3], (NEAR, PMAX, PMAX, NXC, NCELL), 0.15, 0.9, ((3, 128), (4, 4)), jnp.float32),
        "neighbours": draw_neighbours(jax.random.fold_in(arg_keys[6], 71), 0),
        "spectrum": draw_spectrum(jax.random.fold_in(arg_keys[6], 71), 0),
    }


def reference(charges, counts, projection, near_blocks, neighbours, spectrum):
    slot_ids = lax.broadcasted_iota(jnp.int32, charges.shape, 0)
    panel_mask = (slot_ids < counts[None]).astype(jnp.float32)
    masked = charges * panel_mask
    tile_values = jnp.einsum("ptxc,pxc->txc", projection, masked, precision=lax.Precision.HIGHEST)
    grid_field = tile_values.reshape(TX, TY, TZ, NXC, NYC, NZC).transpose(3, 0, 4, 1, 5, 2).reshape(NX, NY, NZ)
    freq = jnp.fft.fftn(grid_field)
    kernel = jnp.transpose(spectrum, (0, 2, 1))
    grid_potential = jnp.real(jnp.fft.ifftn(freq * kernel)).astype(jnp.float32)
    tile_potential = grid_potential.reshape(NXC, TX, NYC, TY, NZC, TZ).transpose(1, 3, 5, 0, 2, 4).reshape(TX * TY * TZ, NXC, NCELL)
    far_field = jnp.einsum("ptxc,txc->pxc", projection, tile_potential, precision=lax.Precision.HIGHEST)
    codes = neighbours.reshape(NEAR, NXC, NYC, NZC).astype(jnp.int32)
    step_x = codes // 9 - 1
    step_y = (codes // 3) % 3 - 1
    step_z = codes % 3 - 1
    plane_ids = lax.broadcasted_iota(jnp.int32, codes.shape, 1)
    row_ids = lax.broadcasted_iota(jnp.int32, codes.shape, 2)
    depth_ids = lax.broadcasted_iota(jnp.int32, codes.shape, 3)
    target = (((plane_ids + step_x) % NXC) * NYC + (row_ids + step_y) % NYC) * NZC + (depth_ids + step_z) % NZC
    picked = jnp.take(masked.reshape(PMAX, NXC * NCELL), target.reshape(-1).astype(jnp.int32), axis=1).reshape(PMAX, NEAR, NXC, NCELL)
    near_field = jnp.einsum("kpqxc,qkxc->pxc", near_blocks, picked, precision=lax.Precision.HIGHEST)
    return (far_field + near_field) * panel_mask
```

```python
import functools

import jax
import jax.numpy as jnp
import numpy as np
from jax import lax
from jax.experimental import pallas as pl
from jax.experimental.pallas import tpu as pltpu
from jax.sharding import PartitionSpec as P

F32 = jnp.float32
BF16 = jnp.bfloat16
NZ_RING = 16
NU = 32
SCALE = 1.0 / 16777216.0
POS_OF_K2 = (0, 2, 1, 3)


def split_np(table):
    hi = table.astype(np.float32).astype(jnp.bfloat16)
    lo = (table - hi.astype(np.float64)).astype(jnp.bfloat16)
    return hi, lo


def cis(num, den):
    ang = 2.0 * np.pi * (num % den) / den
    return np.cos(ang), np.sin(ang)


def slot_freq(z, j):
    return z + 16 * j


def z_table():
    tab = np.zeros((16, 2, 2, 4, 8, 16))
    zc = np.arange(16)
    for z in range(16):
        for j in range(2):
            for tz in range(4):
                gz = zc * 4 + tz
                if z == 0 and j == 0:
                    re, im = np.ones(16), 1.0 - 2.0 * (gz % 2)
                else:
                    c, s = cis(slot_freq(z, j) * gz, 64)
                    re, im = c, -s
                tab[z, 0, j, tz] = re
                tab[z, 1, j, tz] = im
    return tab.reshape(64, 512)


def z_table_wide():
    tab = z_table().reshape(16, 2, 1, 2, 512)
    return np.broadcast_to(tab, (16, 2, 4, 2, 512)).reshape(256, 512)


def y_table():
    r8, ty, l = np.meshgrid(np.arange(8), np.arange(4), np.arange(4), indexing="ij")
    low = (l * 32 + r8 * 4 + ty).reshape(-1)
    k0, u, zq = np.meshgrid(np.arange(4), np.arange(32), np.arange(4), indexing="ij")
    ky = zq * 128 + u * 4 + k0
    c, s = cis(ky[..., None] * low, 512)
    tab = np.zeros((4, 32, 2, 4, 2, 128))
    tab[:, :, 0, :, 0] = c
    tab[:, :, 0, :, 1] = s
    tab[:, :, 1, :, 0] = -s
    tab[:, :, 1, :, 1] = c
    return tab.reshape(4, 256, 256)


def x_table():
    c, s = cis(np.arange(32)[:, None] * np.arange(32)[None, :], 32)
    tab = np.zeros((32, 2, 4, 32, 2, 4))
    for q in range(4):
        tab[:, 0, q, :, 0, q] = c
        tab[:, 0, q, :, 1, q] = s
        tab[:, 1, q, :, 0, q] = -s
        tab[:, 1, q, :, 1, q] = c
    return tab.reshape(256, 256)


def lane_parts():
    lane = np.arange(128)
    return lane // 32, (lane // 8) % 4, (lane // 2) % 4, lane % 2


def twist_table(u_or_k1, second):
    k0, kx0, tx, _ = lane_parts()
    row = np.arange(32)[:, None]
    num = tx[None] * (kx0[None] + 4 * row) if second else 4 * row * kx0[None]
    c, s = cis(num, 512)
    cc = np.zeros((32, 2, 4, 128))
    ss = np.zeros((32, 2, 4, 128))
    cc[:] = c[:, None, None, :]
    ss[:, 0] = s[:, None, :]
    ss[:, 1] = -s[:, None, :]
    return cc.reshape(256, 128).astype(np.float32), ss.reshape(256, 128).astype(np.float32)


def pick_table():
    tab = np.zeros((32, 2, 4, 4, 128))
    for k1 in range(32):
        for q in range(4):
            tab[k1, :, q, q, 4 * k1 : 4 * k1 + 4] = 1.0
    return tab.reshape(256, 512)


@functools.cache
def tables():
    out = []
    zt = z_table()
    out += list(split_np(zt))
    out += list(split_np(y_table()))
    g = x_table()
    out += list(split_np(g))
    out += list(split_np(g.T))
    out += list(twist_table(None, False))
    out += list(twist_table(None, True))
    out.append(pick_table().astype(jnp.bfloat16))
    out += list(split_np(z_table_wide()))
    return tuple(np.asarray(t) for t in out)


def roll(x, shift, axis):
    if axis == 1 and x.shape[1] > 128:
        return jnp.concatenate([roll(x[:, i : i + 128], shift, 1) for i in range(0, x.shape[1], 128)], axis=1)
    return pltpu.roll(x, shift % x.shape[axis], axis)


def sub4(x):
    return roll(x, 4, 0)


def iota(shape, dim):
    return lax.broadcasted_iota(jnp.int32, shape, dim)


def split(x):
    hi = x.astype(BF16)
    return hi, (x - hi.astype(F32)).astype(BF16)


NN = (((1,), (0,)), ((), ()))
NT = (((1,), (1,)), ((), ()))


def dot(a, b, dims):
    return lax.dot_general(a, b, dims, preferred_element_type=F32)


def dot3(ah, al, bh, bl, dims):
    return dot(ah, bh, dims) + (dot(al, bh, dims) + dot(ah, bl, dims))


def four_point(parts, sign):
    (ar, ai), (br, bi), (cr, ci), (dr, di) = parts
    pr, pi, mr, mi = ar + cr, ai + ci, ar - cr, ai - ci
    qr, qi, nr, ni = br + dr, bi + di, br - dr, bi - di
    if sign < 0:
        return [(pr + qr, pi + qi), (mr + ni, mi - nr), (pr - qr, pi - qi), (mr - ni, mi + nr)]
    return [(pr + qr, pi + qi), (mr - ni, mi + nr), (pr - qr, pi - qi), (mr + ni, mi - nr)]


def lane_partner(x, stride, bit):
    return jnp.where(bit == 0, roll(x, -stride, 1), roll(x, stride, 1))


def swap_signed(x, ri, sign):
    r = sub4(x)
    return jnp.where(ri == 0, -r, r) if sign > 0 else jnp.where(ri == 0, r, -r)


def lane_dft4(x, sign):
    lane = iota(x.shape, 1)
    ri = (iota(x.shape, 0) >> 2) & 1
    b1, b0 = (lane >> 2) & 1, (lane >> 1) & 1
    if sign < 0:
        a = lane_partner(x, 4, b1)
        x = jnp.where(b1 == 0, x + a, a - x)
        x = jnp.where((b1 == 1) & (b0 == 1), swap_signed(x, ri, -1), x)
        c = lane_partner(x, 2, b0)
        return jnp.where(b0 == 0, x + c, c - x)
    c = lane_partner(x, 2, b0)
    x = jnp.where(b0 == 0, x + c, c - x)
    x = jnp.where((b1 == 1) & (b0 == 1), swap_signed(x, ri, 1), x)
    a = lane_partner(x, 4, b1)
    return jnp.where(b1 == 0, x + a, a - x)


def masked_charges(ch, cnt):
    row = iota((8, 128), 0)
    return [jnp.where(2 * i + (row >> 2) < cnt, ch(i), 0.0) for i in range(4)]


def both_halves(mv):
    row = iota((8, 128), 0)
    out = []
    for v in mv:
        r = sub4(v)
        out += [jnp.where(row < 4, v, r), jnp.where(row < 4, r, v)]
    return out


def tiles_of(proj, m):
    out = []
    for v in range(32):
        acc = proj(0, v) * m[0]
        for p in range(1, 8):
            acc = acc + proj(p, v) * m[p]
        out.append(acc)
    return out


def regroup(tile):
    low = iota((8, 128), 0) < 4
    base = [[[None] * 4 for _ in range(2)] for _ in range(4)]
    for tx in range(4):
        for a in range(2):
            for h in range(2):
                v0, v1 = tile[tx * 8 + 4 * a + h], tile[tx * 8 + 4 * a + 2 + h]
                base[tx][a][2 * h] = jnp.where(low, v0, sub4(v1))
                base[tx][a][2 * h + 1] = jnp.where(low, sub4(v0), v1)
    return base


def ungroup(e):
    low = iota((8, 128), 0) < 4
    out = [None] * 32
    for tx in range(4):
        for a in range(2):
            for h in range(2):
                p, q = e[tx][a][2 * h], e[tx][a][2 * h + 1]
                out[tx * 8 + 4 * a + h] = jnp.where(low, p, sub4(q))
                out[tx * 8 + 4 * a + 2 + h] = jnp.where(low, sub4(p), q)
    return out


def y_fixup(whole, part, k0, off):
    lane, row = iota(whole.shape, 1), iota(whole.shape, 0)
    zq, ri, u = lane & 3, (lane >> 2) & 1, lane >> 3
    rest = whole - part
    swapped = jnp.where(ri == 0, roll(rest, -4, 1), -roll(rest, 4, 1))
    alone = (u == 0) & ((zq & 1) == 0) if k0 == 0 else (lane < 0)
    special = ((row & 1) + off == 0) & jnp.logical_not(alone)
    return jnp.where(special, jnp.where(zq < 2, part, swapped), whole)


def y_forward(whole, part, fh, fl, off):
    rows = []
    for k0 in range(4):
        x = jnp.concatenate(
            [
                jnp.concatenate([jnp.concatenate(y[k0], axis=0) for y in pair], axis=1)
                for pair in (whole, part)
            ],
            axis=0,
        )
        xh, xl = split(x)
        o = dot3(xh, xl, fh(k0), fl(k0), NT)
        rows.append(y_fixup(o[:32], o[32:], k0, off))
    return jnp.concatenate(rows, axis=0).T


def y_backward(v, fh, fl, off):
    vt = v.T
    first, second = ([], []), ([], [])
    for k0 in range(4):
        a = vt[k0 * 32 : k0 * 32 + 32]
        lane, row = iota(a.shape, 1), iota(a.shape, 0)
        zq, ri, u = lane & 3, (lane >> 2) & 1, lane >> 3
        special = (row & 1) + off == 0
        alone = (u == 0) & ((zq & 1) == 0) if k0 == 0 else (lane < 0)
        va = jnp.where(special & (zq >= 2) & jnp.logical_not(alone), 0.0, a)
        vb = jnp.where(zq >= 2, a, 0.0)
        if k0 == 0:
            vb = jnp.where(alone, jnp.where(ri == 0, roll(a, -4, 1), -roll(a, 4, 1)), vb)
        xh, xl = split(jnp.concatenate([va, vb], axis=0))
        o = dot3(xh, xl, fh(k0), fl(k0), NN)
        for half, pair in enumerate((first, second)):
            for ri_part in range(2):
                pair[ri_part].append(
                    [
                        o[32 * half + 8 * q : 32 * half + 8 * q + 8, 128 * ri_part : 128 * ri_part + 128]
                        for q in range(4)
                    ]
                )
    return first, second


def low_forward(r1):
    inner = [
        four_point([(r1(zh * 4 + zl, 0), r1(zh * 4 + zl, 1)) for zl in range(4)], -1)
        for zh in range(4)
    ]
    yr, yi = [], []
    for k0 in range(4):
        o = four_point([inner[zh][k0] for zh in range(4)], -1)
        yr.append([p[0] for p in o])
        yi.append([p[1] for p in o])
    return yr, yi


def low_backward(y):
    inner = [four_point(list(zip(y[0][k0], y[1][k0])), 1) for k0 in range(4)]
    return [four_point([inner[k0][zh] for k0 in range(4)], 1) for zh in range(4)]


def merge_planes(first, second, off):
    special = (iota((8, 128), 0) & 1) + off == 0
    a, b = low_backward(first), low_backward(second)
    return [
        (a[z // 4][z % 4][0], jnp.where(special, b[z // 4][z % 4][0], a[z // 4][z % 4][1]))
        for z in range(16)
    ]


def twist(x, c, s):
    return x * c + sub4(x) * s


def x_input(r2, tc, ts):
    lane, row = iota((8, 128), 1), iota((8, 128), 0)
    kx0 = (lane >> 3) & 3
    main, conj = [], []
    for u in range(32):
        v = r2(u)
        w = jnp.where(kx0 == 1, roll(v, -16, 1), jnp.where(kx0 == 3, roll(v, 16, 1), v))
        w = jnp.where(row < 4, w, -w)
        main.append(twist(v, tc(u), ts(u)))
        conj.append(twist(w, tc(u), ts(u)))
    return jnp.concatenate(
        [jnp.concatenate(main, axis=0), jnp.concatenate(conj, axis=0)], axis=1
    )


def x_middle(q, k1, tc, ts, c1, c2):
    a = lane_dft4(twist(q[:, :128], tc, ts), -1)
    b = lane_dft4(twist(q[:, 128:], tc, ts), -1)
    return twist(lane_dft4(a * c1 + b * c2, 1), tc, -ts)


def coefficients(sm, sa, off, off_u):
    lane, row = iota((8, 128), 1), iota((8, 128), 0)
    zq = row & 3
    special = (lane >> 5) + (lane & 1) + (zq & 1) + off + off_u == 0
    c1 = jnp.where(special, 0.5 * SCALE * (sm + sa), 2.0 * SCALE * sm)
    half = 0.5 * SCALE * (sm - sa)
    c2 = jnp.where(special, jnp.where(zq < 2, half, -half), 0.0)
    return c1, c2


def spread_spectrum(rows, pick):
    lane = iota((8, 128), 1)
    keep = [(lane & 3) == kx0 for kx0 in range(4)]
    cols = []
    for zq in range(4):
        parts = []
        for alt in range(2):
            b = rows(zq, alt)
            for k0 in range(4):
                for kx0 in range(4):
                    parts.append(jnp.where(keep[kx0], b[8 * k0 : 8 * k0 + 8], 0.0))
        cols.append(jnp.concatenate(parts, axis=0))
    m = jnp.concatenate(cols, axis=1)
    h, l = split(m)
    return dot(pick, h, NT) + dot(pick, l, NT)


def z_backward_fold(o):
    lane = iota((8, 128), 1)
    e = [[[None] * 4 for _ in range(2)] for _ in range(4)]
    for tx in range(4):
        for a in range(2):
            for tz in range(4):
                acc = o(tx, 0, a, tz)
                for r8 in range(1, 8):
                    acc = jnp.where((lane >> 4) == r8, o(tx, r8, a, tz), acc)
                e[tx][a][tz] = acc
    return e


def far_of(proj, pot):
    out = []
    for p in range(8):
        acc = proj(p, 0) * pot[0]
        for v in range(1, 32):
            acc = acc + proj(p, v) * pot[v]
        out.append(acc)
    return out


def near_of(plane, above, below, codes, near):
    lane, row = iota((8, 128), 1), iota((8, 128), 0)
    l, zc = row & 3, lane & 15
    code = [codes(k) for k in range(6)]
    picked = [[jnp.zeros((8, 128), F32)] * 4 for _ in range(6)]
    for d in range(3):
        for i in range(4):
            v = plane(d, i)
            up = roll(v, -16, 1)
            nxt = jnp.where(l == 3, roll(below(d, i), -16, 1), roll(up, -1, 0))
            after = jnp.where(lane >= 112, nxt, up)
            dn = roll(v, 16, 1)
            prv = jnp.where(l == 0, roll(above(d, i), 16, 1), roll(dn, 1, 0))
            before = jnp.where(lane < 16, prv, dn)
            for e, w in enumerate((before, v, after)):
                plus = jnp.where(zc == 15, roll(w, 15, 1), roll(w, -1, 1))
                minus = jnp.where(zc == 0, roll(w, -15, 1), roll(w, 1, 1))
                for f, x in enumerate((minus, w, plus)):
                    for k in range(6):
                        if k == 0 and (d, e, f) != (1, 1, 1):
                            continue
                        if k > 0 and (d, e, f) == (1, 1, 1):
                            continue
                        picked[k][i] = (
                            x if k == 0 else jnp.where(code[k] == 9 * d + 3 * e + f, x, picked[k][i])
                        )
    out = []
    for p in range(8):
        acc = None
        for k in range(6):
            for i in range(4):
                t = near(k, p, i) * picked[k][i]
                acc = t if acc is None else acc + t
        out.append(acc)
    return out


def z_order():
    out = []
    for step in range(8, 0, -1):
        out += [step] if step == 8 else [step, 16 - step]
    return out


def u_order():
    far = (0, 1, 2, 1)
    out = [(x, y, c) for x in range(4) for y in range(4) for c in range(2)]
    out.remove((0, 0, 0))
    return sorted(out, key=lambda t: (-far[t[0]] - far[t[1]], t))


def body(
    ch,
    cnt,
    proj,
    near,
    nbr,
    spec,
    *rest,
):
    tab_in, (out,), scr = rest[:15], rest[15:16], rest[16:]
    tab = scr[:15]
    (ch_s, cnt_s, proj_s, near_s, nbr_s) = scr[15:20]
    (sp, bm, nd, tp_h, tp_l) = scr[20:25]
    (s1, r1, s2, r2, s3, r3, s4, r4) = scr[25:33]
    (ms, bf, bl, hp, ha, hb, cc) = scr[33:40]
    (in_sem, tab_sem, loc_sem, snd, rcv) = scr[40:]
    (wzh, wzl, fh, fl, gh, gl, gth, gtl, t1c, t1s, t2c, t2s, pick, wxh, wxl) = tab

    slab, zl = lax.axis_index("slab"), lax.axis_index("cell")
    slabs = lax.axis_size("slab")
    zh, u = slab // NU, slab % NU
    z = zh * 4 + zl
    off = z
    off_u = u

    def z_peer(d):
        t = (z + d) % 16
        return t, ((t // 4) * NU + u, t % 4)

    def u_peer(d):
        t = ((u // 8 + d[0]) % 4) * 8 + ((u // 2 % 4 + d[1]) % 4) * 2 + (u + d[2]) % 2
        return t, (zh * NU + t, zl)

    def near_peer(e, f):
        return ((slab + slabs + e) % slabs, (zl + 4 + f) % 4)

    halo = [(e, f) for e in (-1, 0, 1) for f in (-1, 0, 1) if (e, f) != (0, 0)]

    first = [
        pltpu.make_async_copy(a, b, in_sem.at[i])
        for i, (a, b) in enumerate(
            ((ch, ch_s), (cnt, cnt_s), (proj, proj_s), (nbr, nbr_s), (near, near_s))
        )
    ]
    load = [pltpu.make_async_copy(a, b, tab_sem.at[i]) for i, (a, b) in enumerate(zip(tab_in, tab))]
    for c in first[:3] + load[:2]:
        c.start()

    barrier = pltpu.get_barrier_semaphore()
    peers = [z_peer(d)[1] for d in z_order()] + [u_peer(d)[1] for d in u_order()]
    peers += [near_peer(e, f) for e, f in halo]
    for p in peers:
        pl.semaphore_signal(barrier, inc=1, device_id=p, device_id_type=pl.DeviceIdType.MESH)
    for c in load[2:] + first[3:]:
        c.start()
    own = [
        pltpu.make_async_copy(spec.at[z + 16 * j], sp.at[zh, j], loc_sem.at[j]) for j in range(3)
    ]
    for c in own:
        c.start()

    def send(src, dst, i, dev):
        pltpu.make_async_remote_copy(
            src_ref=src,
            dst_ref=dst,
            send_sem=snd.at[i],
            recv_sem=rcv.at[i],
            device_id=dev,
            device_id_type=pl.DeviceIdType.MESH,
        ).start()

    def done(sem, i, ref):
        pltpu.make_async_copy(ref, ref, sem.at[i]).wait()

    first[0].wait()
    first[1].wait()
    half = cnt_s[...]
    cc[0:4, :] = half
    cc[4:8, :] = half
    mv = masked_charges(lambda i: ch_s[8 * i : 8 * i + 8, :], cc[...])
    for i in range(4):
        ms[8 * i : 8 * i + 8, :] = mv[i]
        for h in range(2):
            bf[2 * i + h : 2 * i + h + 1, :] = mv[i][4 * h : 4 * h + 1]
            bl[2 * i + h : 2 * i + h + 1, :] = mv[i][4 * h + 3 : 4 * h + 4]
    m = both_halves(mv)
    first[2].wait()

    def proj_at(p, v):
        r = (p * 32 + v) * 8
        return proj_s[r : r + 8, :]

    base = regroup(tiles_of(proj_at, m))
    lane16 = iota((16, 128), 1)
    keep = [jnp.where((lane16 >> 4) == r8, 1.0, 0.0).astype(BF16) for r8 in range(8)]
    for tx in range(4):
        for tz in range(4):
            h, l = split(jnp.concatenate([base[tx][0][tz], base[tx][1][tz]], axis=0))
            for r8 in range(8):
                r = tx * 128 + r8 * 16
                tp_h[r : r + 16, tz * 128 : tz * 128 + 128] = h * keep[r8]
                tp_l[r : r + 16, tz * 128 : tz * 128 + 128] = l * keep[r8]
    load[0].wait()
    load[1].wait()
    o = dot3(wzh[...], wzl[...], tp_h[...], tp_l[...], NT)
    for t in range(16):
        for ri in range(2):
            for tx in range(4):
                r = t * 4 + ri * 2
                s1[t, ri, 2 * tx : 2 * tx + 2, :] = o[r : r + 2, tx * 128 : tx * 128 + 128]
    pl.semaphore_wait(barrier, len(peers))
    for d in z_order():
        t, dev = z_peer(d)
        send(s1.at[t], r1.at[z], 0, dev)
    r1[pl.ds(z, 1)] = s1[pl.ds(z, 1)]

    for d in (2, 1, 3):
        th = (zh + d) % 4
        dev = (th * NU + u, zl)
        tz_id = th * 4 + zl
        for j in range(2):
            send(spec.at[tz_id + 16 * j], sp.at[zh, j], 4, dev)

        @pl.when(tz_id == 0)
        def _():
            send(spec.at[tz_id + 32], sp.at[zh, 2], 5, dev)

    for e, f in halo:
        dev = near_peer(e, f)
        if f == 0:
            send(ms, hp.at[(1 - e) // 2], 6 + (1 - e) // 2, dev)
        elif f == 1:
            send(bl, ha.at[1 - e], 8, dev)
        else:
            send(bf, hb.at[1 - e], 9, dev)

    for i in (2, 3):
        load[i].wait()
    done(rcv, 0, s1.at[pl.ds(0, 15)])

    zero = jnp.zeros((8, 128), F32)
    whole = low_forward(lambda t, ri: r1[t, ri])
    part = low_forward(lambda t, ri: zero if ri else r1[t, 0])
    y = y_forward(whole, part, lambda k: fh[k], lambda k: fl[k], off)
    for t in range(32):
        s2[t] = y[8 * t : 8 * t + 8]
    for d in u_order():
        t, dev = u_peer(d)
        send(s2.at[t], r2.at[u], 1, dev)
    r2[pl.ds(u, 1)] = s2[pl.ds(u, 1)]

    for i in range(4, 15):
        load[i].wait()
    for c in own:
        c.wait()
    done(rcv, 4, sp.at[pl.ds(0, 3), pl.ds(0, 2)])

    @pl.when(z == 0)
    def _():
        done(rcv, 5, sp.at[pl.ds(0, 3), 0])

    packed = jnp.where(z == 0, 2, 0)
    for zq in range(4):
        for alt in range(2):
            src = (packed if (zq >= 2) != (alt == 1) else 0, 1)
            for k0 in range(4):
                for pos in range(4):
                    k2 = POS_OF_K2.index(pos)
                    for j in range(2):
                        r = k0 * 8 + pos * 2 + j
                        bm[zq, alt, r : r + 1, :] = sp[
                            zq, src[j], k0 : k0 + 1, k2 * 128 : k2 * 128 + 128
                        ]
    sm = spread_spectrum(lambda zq, alt: bm[zq, alt], pick[...])

    done(rcv, 1, s2.at[pl.ds(0, 31)])

    def rows8(ref):
        return lambda i: ref[8 * i : 8 * i + 8, :]

    xh, xl = split(x_input(lambda t: r2[t], rows8(t1c), rows8(t1s)))
    q = dot3(gh[...], gl[...], xh, xl, NN)
    ws = []
    for k1 in range(32):
        a = slice(8 * k1, 8 * k1 + 8)
        c1, c2 = coefficients(sm[a, :128], sm[a, 128:], off, off_u)
        ws.append(x_middle(q[a], k1, t2c[a, :], t2s[a, :], c1, c2))
    xh, xl = split(jnp.concatenate(ws, axis=0))
    o = dot3(gth[...], gtl[...], xh, xl, NN)
    for t in range(32):
        a = slice(8 * t, 8 * t + 8)
        s3[t] = twist(o[a], t1c[a, :], -t1s[a, :])
    for d in u_order():
        t, dev = u_peer(d)
        send(s3.at[t], r3.at[u], 2, dev)
    r3[pl.ds(u, 1)] = s3[pl.ds(u, 1)]
    done(rcv, 2, s3.at[pl.ds(0, 31)])

    v = jnp.concatenate([r3[t] for t in range(32)], axis=0)
    first_part, second_part = y_backward(v, lambda k: fh[k], lambda k: fl[k], off)
    blocks = merge_planes(first_part, second_part, off)
    for t in range(16):
        for ri in range(2):
            s4[t, ri] = blocks[t][ri]
    for d in z_order():
        t, dev = z_peer(d)
        send(s4.at[t], r4.at[z], 3, dev)
    r4[pl.ds(z, 1)] = s4[pl.ds(z, 1)]

    first[3].wait()
    first[4].wait()
    for k in range(6):
        half = nbr_s[4 * k : 4 * k + 4, :]
        nd[k, 0:4, :] = half
        nd[k, 4:8, :] = half
    done(rcv, 6, hp.at[0])
    done(rcv, 7, hp.at[0])
    done(rcv, 8, ha)
    done(rcv, 9, hb)

    def plane(d, i):
        a = slice(8 * i, 8 * i + 8)
        return ms[a, :] if d == 1 else hp[d // 2, a, :]

    low = iota((8, 128), 0) < 4

    def edge(ref):
        def get(d, i):
            pair = ref[d, 2 * i : 2 * i + 2, :]
            return jnp.where(
                low,
                jnp.broadcast_to(pair[0:1], (8, 128)),
                jnp.broadcast_to(pair[1:2], (8, 128)),
            )

        return get

    def near_at(k, p, i):
        r = ((k * 8 + p) * 4 + i) * 8
        return near_s[r : r + 8, :]

    near_sum = near_of(plane, edge(ha), edge(hb), lambda k: nd[k], near_at)

    done(rcv, 3, s4.at[pl.ds(0, 15)])

    rt = jnp.concatenate([r4[t, ri] for t in range(16) for ri in range(2)], axis=0).T
    th, tl = split(rt)
    xs_h, xs_l = [], []
    for tx in range(4):
        mk = jnp.where(((lane16 >> 1) & 3) == tx, 1.0, 0.0).astype(BF16)
        mk = jnp.concatenate([jnp.concatenate([mk, mk], axis=1)] * 8, axis=0)
        xs_h.append(th * mk)
        xs_l.append(tl * mk)
    o = dot3(jnp.concatenate(xs_h, axis=0), jnp.concatenate(xs_l, axis=0), wxh[...], wxl[...], NN)

    def o_at(tx, r8, a, tz):
        r = tx * 128 + r8 * 16 + a * 8
        return o[r : r + 8, tz * 128 : tz * 128 + 128]

    far = far_of(proj_at, ungroup(z_backward_fold(o_at)))
    row = iota((8, 128), 0)
    both = cc[...]
    for i in range(4):
        a, b = far[2 * i] + near_sum[2 * i], far[2 * i + 1] + near_sum[2 * i + 1]
        tot = jnp.where(low, a + sub4(a), b + sub4(b))
        out[8 * i : 8 * i + 8, :] = jnp.where(2 * i + (row >> 2) < both, tot, 0.0)

    done(snd, 0, s1.at[pl.ds(0, 15)])
    done(snd, 1, s2.at[pl.ds(0, 31)])
    done(snd, 2, s3.at[pl.ds(0, 31)])
    done(snd, 3, s4.at[pl.ds(0, 15)])
    done(snd, 4, sp.at[pl.ds(0, 3), pl.ds(0, 2)])

    for d in (2, 1, 3):

        @pl.when(((zh + d) % 4) * 4 + zl == 0)
        def _():
            done(snd, 5, sp.at[0, 0])

    done(snd, 6, ms)
    done(snd, 7, ms)
    done(snd, 8, ha)
    done(snd, 9, hb)


def per_device(charges, counts, projection, near_blocks, neighbours, spectrum):
    tabs = [jnp.asarray(t) for t in tables()]
    ins = [
        charges.reshape(32, 128),
        counts.reshape(4, 128),
        projection.reshape(2048, 128),
        near_blocks.reshape(1536, 128),
        neighbours.reshape(24, 128),
        jnp.transpose(spectrum, (1, 2, 0)),
    ]
    vm = pltpu.VMEM
    scratch = [vm(t.shape, t.dtype) for t in tabs]
    scratch += [vm(a.shape, a.dtype) for a in ins[:5]]
    scratch += [
        vm((4, 3, 4, 512), F32),
        vm((4, 2, 32, 128), F32),
        vm((6, 8, 128), jnp.int32),
        vm((512, 512), BF16),
        vm((512, 512), BF16),
    ]
    scratch += [vm((16, 2, 8, 128), F32)] * 2 + [vm((32, 8, 128), F32)] * 4
    scratch += [vm((16, 2, 8, 128), F32)] * 2
    scratch += [
        vm((32, 128), F32),
        vm((8, 128), F32),
        vm((8, 128), F32),
        vm((2, 32, 128), F32),
        vm((3, 8, 128), F32),
        vm((3, 8, 128), F32),
        vm((8, 128), jnp.int32),
    ]
    dma = pltpu.SemaphoreType.DMA
    scratch += [dma((5,)), dma((15,)), dma((3,)), dma((10,)), dma((10,))]
    res = pl.pallas_call(
        body,
        out_shape=jax.ShapeDtypeStruct((32, 128), F32),
        in_specs=[pl.BlockSpec(memory_space=pl.ANY)] * (6 + len(tabs)),
        out_specs=pl.BlockSpec(memory_space=pltpu.VMEM),
        scratch_shapes=scratch,
        compiler_params=pltpu.CompilerParams(
            collective_id=0, has_side_effects=True, vmem_limit_bytes=48 << 20
        ),
        name="potential",
    )(*ins, *tabs)
    return res.reshape(8, 1, 512)


def solution(mesh):
    in_specs = (
        P(None, "slab", "cell"),
        P("slab", "cell"),
        P(None, None, "slab", "cell"),
        P(None, None, None, "slab", "cell"),
        P(None, "slab", "cell"),
        P(None, None, "slab"),
    )
    return jax.shard_map(
        per_device, mesh=mesh, in_specs=in_specs, out_specs=P(None, "slab", "cell"), check_vma=False
    )
```

```python
import functools

import jax
import jax.numpy as jnp
import numpy as np
from jax import lax
from jax.experimental import pallas as pl
from jax.experimental.pallas import tpu as pltpu
from jax.sharding import PartitionSpec as P

F32 = jnp.float32
BF16 = jnp.bfloat16
NZ_RING = 16
NU = 32
SCALE = 1.0 / 16777216.0
POS_OF_K2 = (0, 2, 1, 3)


def split_np(table):
    hi = table.astype(np.float32).astype(jnp.bfloat16)
    lo = (table - hi.astype(np.float64)).astype(jnp.bfloat16)
    return hi, lo


def cis(num, den):
    ang = 2.0 * np.pi * (num % den) / den
    return np.cos(ang), np.sin(ang)


def slot_freq(z, j):
    return z + 16 * j


def z_table():
    tab = np.zeros((16, 2, 2, 4, 8, 16))
    zc = np.arange(16)
    for z in range(16):
        for j in range(2):
            for tz in range(4):
                gz = zc * 4 + tz
                if z == 0 and j == 0:
                    re, im = np.ones(16), 1.0 - 2.0 * (gz % 2)
                else:
                    c, s = cis(slot_freq(z, j) * gz, 64)
                    re, im = c, -s
                tab[z, 0, j, tz] = re
                tab[z, 1, j, tz] = im
    return tab.reshape(64, 512)


def z_table_wide():
    tab = z_table().reshape(16, 2, 1, 2, 512)
    return np.broadcast_to(tab, (16, 2, 4, 2, 512)).reshape(256, 512)


def y_table():
    r8, ty, l = np.meshgrid(np.arange(8), np.arange(4), np.arange(4), indexing="ij")
    low = (l * 32 + r8 * 4 + ty).reshape(-1)
    k0, u, zq = np.meshgrid(np.arange(4), np.arange(32), np.arange(4), indexing="ij")
    ky = zq * 128 + u * 4 + k0
    c, s = cis(ky[..., None] * low, 512)
    tab = np.zeros((4, 32, 2, 4, 2, 128))
    tab[:, :, 0, :, 0] = c
    tab[:, :, 0, :, 1] = s
    tab[:, :, 1, :, 0] = -s
    tab[:, :, 1, :, 1] = c
    return tab.reshape(4, 256, 256)


def x_table():
    c, s = cis(np.arange(32)[:, None] * np.arange(32)[None, :], 32)
    tab = np.zeros((32, 2, 4, 32, 2, 4))
    for q in range(4):
        tab[:, 0, q, :, 0, q] = c
        tab[:, 0, q, :, 1, q] = s
        tab[:, 1, q, :, 0, q] = -s
        tab[:, 1, q, :, 1, q] = c
    return tab.reshape(256, 256)


def lane_parts():
    lane = np.arange(128)
    return lane // 32, (lane // 8) % 4, (lane // 2) % 4, lane % 2


def twist_table(u_or_k1, second):
    k0, kx0, tx, _ = lane_parts()
    row = np.arange(32)[:, None]
    num = tx[None] * (kx0[None] + 4 * row) if second else 4 * row * kx0[None]
    c, s = cis(num, 512)
    cc = np.zeros((32, 2, 4, 128))
    ss = np.zeros((32, 2, 4, 128))
    cc[:] = c[:, None, None, :]
    ss[:, 0] = s[:, None, :]
    ss[:, 1] = -s[:, None, :]
    return cc.reshape(256, 128).astype(np.float32), ss.reshape(256, 128).astype(np.float32)


def pick_table():
    tab = np.zeros((32, 2, 4, 4, 128))
    for k1 in range(32):
        for q in range(4):
            tab[k1, :, q, q, 4 * k1 : 4 * k1 + 4] = 1.0
    return tab.reshape(256, 512)


@functools.cache
def tables():
    out = []
    zt = z_table()
    out += list(split_np(zt))
    out += list(split_np(y_table()))
    g = x_table()
    out += list(split_np(g))
    out += list(split_np(g.T))
    out += list(twist_table(None, False))
    out += list(twist_table(None, True))
    out.append(pick_table().astype(jnp.bfloat16))
    out += list(split_np(z_table_wide()))
    return tuple(np.asarray(t) for t in out)


def roll(x, shift, axis):
    if axis == 1 and x.shape[1] > 128:
        return jnp.concatenate([roll(x[:, i : i + 128], shift, 1) for i in range(0, x.shape[1], 128)], axis=1)
    return pltpu.roll(x, shift % x.shape[axis], axis)


def sub4(x):
    return roll(x, 4, 0)


def iota(shape, dim):
    return lax.broadcasted_iota(jnp.int32, shape, dim)


def split(x):
    hi = x.astype(BF16)
    return hi, (x - hi.astype(F32)).astype(BF16)


NN = (((1,), (0,)), ((), ()))
NT = (((1,), (1,)), ((), ()))


def dot(a, b, dims):
    return lax.dot_general(a, b, dims, preferred_element_type=F32)


def dot3(ah, al, bh, bl, dims):
    return dot(ah, bh, dims) + (dot(al, bh, dims) + dot(ah, bl, dims))


def four_point(parts, sign):
    (ar, ai), (br, bi), (cr, ci), (dr, di) = parts
    pr, pi, mr, mi = ar + cr, ai + ci, ar - cr, ai - ci
    qr, qi, nr, ni = br + dr, bi + di, br - dr, bi - di
    if sign < 0:
        return [(pr + qr, pi + qi), (mr + ni, mi - nr), (pr - qr, pi - qi), (mr - ni, mi + nr)]
    return [(pr + qr, pi + qi), (mr - ni, mi + nr), (pr - qr, pi - qi), (mr + ni, mi - nr)]


def lane_partner(x, stride, bit):
    return jnp.where(bit == 0, roll(x, -stride, 1), roll(x, stride, 1))


def swap_signed(x, ri, sign):
    r = sub4(x)
    return jnp.where(ri == 0, -r, r) if sign > 0 else jnp.where(ri == 0, r, -r)


def lane_dft4(x, sign):
    lane = iota(x.shape, 1)
    ri = (iota(x.shape, 0) >> 2) & 1
    b1, b0 = (lane >> 2) & 1, (lane >> 1) & 1
    if sign < 0:
        a = lane_partner(x, 4, b1)
        x = jnp.where(b1 == 0, x + a, a - x)
        x = jnp.where((b1 == 1) & (b0 == 1), swap_signed(x, ri, -1), x)
        c = lane_partner(x, 2, b0)
        return jnp.where(b0 == 0, x + c, c - x)
    c = lane_partner(x, 2, b0)
    x = jnp.where(b0 == 0, x + c, c - x)
    x = jnp.where((b1 == 1) & (b0 == 1), swap_signed(x, ri, 1), x)
    a = lane_partner(x, 4, b1)
    return jnp.where(b1 == 0, x + a, a - x)


def masked_charges(ch, cnt):
    row = iota((8, 128), 0)
    return [jnp.where(2 * i + (row >> 2) < cnt, ch(i), 0.0) for i in range(4)]


def both_halves(mv):
    row = iota((8, 128), 0)
    out = []
    for v in mv:
        r = sub4(v)
        out += [jnp.where(row < 4, v, r), jnp.where(row < 4, r, v)]
    return out


def tiles_of(proj, m):
    out = []
    for v in range(32):
        acc = proj(0, v) * m[0]
        for p in range(1, 8):
            acc = acc + proj(p, v) * m[p]
        out.append(acc)
    return out


def regroup(tile):
    low = iota((8, 128), 0) < 4
    base = [[[None] * 4 for _ in range(2)] for _ in range(4)]
    for tx in range(4):
        for a in range(2):
            for h in range(2):
                v0, v1 = tile[tx * 8 + 4 * a + h], tile[tx * 8 + 4 * a + 2 + h]
                base[tx][a][2 * h] = jnp.where(low, v0, sub4(v1))
                base[tx][a][2 * h + 1] = jnp.where(low, sub4(v0), v1)
    return base


def ungroup(e):
    low = iota((8, 128), 0) < 4
    out = [None] * 32
    for tx in range(4):
        for a in range(2):
            for h in range(2):
                p, q = e[tx][a][2 * h], e[tx][a][2 * h + 1]
                out[tx * 8 + 4 * a + h] = jnp.where(low, p, sub4(q))
                out[tx * 8 + 4 * a + 2 + h] = jnp.where(low, sub4(p), q)
    return out


def y_fixup(whole, part, k0, off):
    lane, row = iota(whole.shape, 1), iota(whole.shape, 0)
    zq, ri, u = lane & 3, (lane >> 2) & 1, lane >> 3
    rest = whole - part
    swapped = jnp.where(ri == 0, roll(rest, -4, 1), -roll(rest, 4, 1))
    alone = (u == 0) & ((zq & 1) == 0) if k0 == 0 else (lane < 0)
    special = ((row & 1) + off == 0) & jnp.logical_not(alone)
    return jnp.where(special, jnp.where(zq < 2, part, swapped), whole)


def y_forward(whole, part, fh, fl, off):
    rows = []
    for k0 in range(4):
        x = jnp.concatenate(
            [
                jnp.concatenate([jnp.concatenate(y[k0], axis=0) for y in pair], axis=1)
                for pair in (whole, part)
            ],
            axis=0,
        )
        xh, xl = split(x)
        o = dot3(xh, xl, fh(k0), fl(k0), NT)
        rows.append(y_fixup(o[:32], o[32:], k0, off))
    return jnp.concatenate(rows, axis=0).T


def y_backward(v, fh, fl, off):
    vt = v.T
    first, second = ([], []), ([], [])
    for k0 in range(4):
        a = vt[k0 * 32 : k0 * 32 + 32]
        lane, row = iota(a.shape, 1), iota(a.shape, 0)
        zq, ri, u = lane & 3, (lane >> 2) & 1, lane >> 3
        special = (row & 1) + off == 0
        alone = (u == 0) & ((zq & 1) == 0) if k0 == 0 else (lane < 0)
        va = jnp.where(special & (zq >= 2) & jnp.logical_not(alone), 0.0, a)
        vb = jnp.where(zq >= 2, a, 0.0)
        if k0 == 0:
            vb = jnp.where(alone, jnp.where(ri == 0, roll(a, -4, 1), -roll(a, 4, 1)), vb)
        xh, xl = split(jnp.concatenate([va, vb], axis=0))
        o = dot3(xh, xl, fh(k0), fl(k0), NN)
        for half, pair in enumerate((first, second)):
            for ri_part in range(2):
                pair[ri_part].append(
                    [
                        o[32 * half + 8 * q : 32 * half + 8 * q + 8, 128 * ri_part : 128 * ri_part + 128]
                        for q in range(4)
                    ]
                )
    return first, second


def low_forward(r1):
    inner = [
        four_point([(r1(zh * 4 + zl, 0), r1(zh * 4 + zl, 1)) for zl in range(4)], -1)
        for zh in range(4)
    ]
    yr, yi = [], []
    for k0 in range(4):
        o = four_point([inner[zh][k0] for zh in range(4)], -1)
        yr.append([p[0] for p in o])
        yi.append([p[1] for p in o])
    return yr, yi


def low_backward(y):
    inner = [four_point(list(zip(y[0][k0], y[1][k0])), 1) for k0 in range(4)]
    return [four_point([inner[k0][zh] for k0 in range(4)], 1) for zh in range(4)]


def merge_planes(first, second, off):
    special = (iota((8, 128), 0) & 1) + off == 0
    a, b = low_backward(first), low_backward(second)
    return [
        (a[z // 4][z % 4][0], jnp.where(special, b[z // 4][z % 4][0], a[z // 4][z % 4][1]))
        for z in range(16)
    ]


def twist(x, c, s):
    return x * c + sub4(x) * s


def x_input(r2, tc, ts):
    lane, row = iota((8, 128), 1), iota((8, 128), 0)
    kx0 = (lane >> 3) & 3
    main, conj = [], []
    for u in range(32):
        v = r2(u)
        w = jnp.where(kx0 == 1, roll(v, -16, 1), jnp.where(kx0 == 3, roll(v, 16, 1), v))
        w = jnp.where(row < 4, w, -w)
        main.append(twist(v, tc(u), ts(u)))
        conj.append(twist(w, tc(u), ts(u)))
    return jnp.concatenate(
        [jnp.concatenate(main, axis=0), jnp.concatenate(conj, axis=0)], axis=1
    )


def x_middle(q, k1, tc, ts, c1, c2):
    a = lane_dft4(twist(q[:, :128], tc, ts), -1)
    b = lane_dft4(twist(q[:, 128:], tc, ts), -1)
    return twist(lane_dft4(a * c1 + b * c2, 1), tc, -ts)


def coefficients(sm, sa, off, off_u):
    lane, row = iota((8, 128), 1), iota((8, 128), 0)
    zq = row & 3
    special = (lane >> 5) + (lane & 1) + (zq & 1) + off + off_u == 0
    c1 = jnp.where(special, 0.5 * SCALE * (sm + sa), 2.0 * SCALE * sm)
    half = 0.5 * SCALE * (sm - sa)
    c2 = jnp.where(special, jnp.where(zq < 2, half, -half), 0.0)
    return c1, c2


def spread_spectrum(rows, pick):
    lane = iota((8, 128), 1)
    keep = [(lane & 3) == kx0 for kx0 in range(4)]
    cols = []
    for zq in range(4):
        parts = []
        for alt in range(2):
            b = rows(zq, alt)
            for k0 in range(4):
                for kx0 in range(4):
                    parts.append(jnp.where(keep[kx0], b[8 * k0 : 8 * k0 + 8], 0.0))
        cols.append(jnp.concatenate(parts, axis=0))
    m = jnp.concatenate(cols, axis=1)
    h, l = split(m)
    return dot(pick, h, NT) + dot(pick, l, NT)


def z_backward_fold(o):
    lane = iota((8, 128), 1)
    e = [[[None] * 4 for _ in range(2)] for _ in range(4)]
    for tx in range(4):
        for a in range(2):
            for tz in range(4):
                acc = o(tx, 0, a, tz)
                for r8 in range(1, 8):
                    acc = jnp.where((lane >> 4) == r8, o(tx, r8, a, tz), acc)
                e[tx][a][tz] = acc
    return e


def far_of(proj, pot):
    out = []
    for p in range(8):
        acc = proj(p, 0) * pot[0]
        for v in range(1, 32):
            acc = acc + proj(p, v) * pot[v]
        out.append(acc)
    return out


def near_of(plane, above, below, codes, near):
    lane, row = iota((8, 128), 1), iota((8, 128), 0)
    l, zc = row & 3, lane & 15
    code = [codes(k) for k in range(6)]
    picked = [[jnp.zeros((8, 128), F32)] * 4 for _ in range(6)]
    for d in range(3):
        for i in range(4):
            v = plane(d, i)
            up = roll(v, -16, 1)
            nxt = jnp.where(l == 3, roll(below(d, i), -16, 1), roll(up, -1, 0))
            after = jnp.where(lane >= 112, nxt, up)
            dn = roll(v, 16, 1)
            prv = jnp.where(l == 0, roll(above(d, i), 16, 1), roll(dn, 1, 0))
            before = jnp.where(lane < 16, prv, dn)
            for e, w in enumerate((before, v, after)):
                plus = jnp.where(zc == 15, roll(w, 15, 1), roll(w, -1, 1))
                minus = jnp.where(zc == 0, roll(w, -15, 1), roll(w, 1, 1))
                for f, x in enumerate((minus, w, plus)):
                    for k in range(6):
                        if k == 0 and (d, e, f) != (1, 1, 1):
                            continue
                        if k > 0 and (d, e, f) == (1, 1, 1):
                            continue
                        picked[k][i] = (
                            x if k == 0 else jnp.where(code[k] == 9 * d + 3 * e + f, x, picked[k][i])
                        )
    out = []
    for p in range(8):
        acc = None
        for k in range(6):
            for i in range(4):
                t = near(k, p, i) * picked[k][i]
                acc = t if acc is None else acc + t
        out.append(acc)
    return out


def z_order():
    out = []
    for step in range(8, 0, -1):
        out += [step] if step == 8 else [step, 16 - step]
    return out


def u_order():
    far = (0, 1, 2, 1)
    out = [(x, y, c) for x in range(4) for y in range(4) for c in range(2)]
    out.remove((0, 0, 0))
    return sorted(out, key=lambda t: (-far[t[0]] - far[t[1]], t))


def body(
    ch,
    cnt,
    proj,
    near,
    nbr,
    spec,
    *rest,
):
    tab_in, (out,), scr = rest[:15], rest[15:16], rest[16:]
    tab = scr[:15]
    (ch_s, cnt_s, proj_s, near_s, nbr_s) = scr[15:20]
    (sp, bm, nd, tp_h, tp_l) = scr[20:25]
    (s1, r1, s2, r2, s3, r3, s4, r4) = scr[25:33]
    (ms, bf, bl, hp, ha, hb, cc) = scr[33:40]
    (in_sem, tab_sem, loc_sem, snd, rcv) = scr[40:]
    (wzh, wzl, fh, fl, gh, gl, gth, gtl, t1c, t1s, t2c, t2s, pick, wxh, wxl) = tab

    slab, zl = lax.axis_index("slab"), lax.axis_index("cell")
    slabs = lax.axis_size("slab")
    zh, u = slab // NU, slab % NU
    z = zh * 4 + zl
    off = z
    off_u = u

    def z_peer(d):
        t = (z + d) % 16
        return t, ((t // 4) * NU + u, t % 4)

    def u_peer(d):
        t = ((u // 8 + d[0]) % 4) * 8 + ((u // 2 % 4 + d[1]) % 4) * 2 + (u + d[2]) % 2
        return t, (zh * NU + t, zl)

    def near_peer(e, f):
        return ((slab + slabs + e) % slabs, (zl + 4 + f) % 4)

    halo = [(e, f) for e in (-1, 0, 1) for f in (-1, 0, 1) if (e, f) != (0, 0)]

    first = [
        pltpu.make_async_copy(a, b, in_sem.at[i])
        for i, (a, b) in enumerate(
            ((ch, ch_s), (cnt, cnt_s), (proj, proj_s), (nbr, nbr_s), (near, near_s))
        )
    ]
    load = [pltpu.make_async_copy(a, b, tab_sem.at[i]) for i, (a, b) in enumerate(zip(tab_in, tab))]
    for c in first[:3] + load[:2]:
        c.start()

    barrier = pltpu.get_barrier_semaphore()
    peers = [z_peer(d)[1] for d in z_order()] + [u_peer(d)[1] for d in u_order()]
    peers += [near_peer(e, f) for e, f in halo]
    for p in peers:
        pl.semaphore_signal(barrier, inc=1, device_id=p, device_id_type=pl.DeviceIdType.MESH)
    for c in load[2:] + first[3:]:
        c.start()
    own = [
        pltpu.make_async_copy(spec.at[z + 16 * j], sp.at[zh, j], loc_sem.at[j]) for j in range(3)
    ]
    for c in own:
        c.start()

    def send(src, dst, i, dev):
        pltpu.make_async_remote_copy(
            src_ref=src,
            dst_ref=dst,
            send_sem=snd.at[i],
            recv_sem=rcv.at[i],
            device_id=dev,
            device_id_type=pl.DeviceIdType.MESH,
        ).start()

    def done(sem, i, ref):
        pltpu.make_async_copy(ref, ref, sem.at[i]).wait()

    first[0].wait()
    first[1].wait()
    half = cnt_s[...]
    cc[0:4, :] = half
    cc[4:8, :] = half
    mv = masked_charges(lambda i: ch_s[8 * i : 8 * i + 8, :], cc[...])
    for i in range(4):
        ms[8 * i : 8 * i + 8, :] = mv[i]
        for h in range(2):
            bf[2 * i + h : 2 * i + h + 1, :] = mv[i][4 * h : 4 * h + 1]
            bl[2 * i + h : 2 * i + h + 1, :] = mv[i][4 * h + 3 : 4 * h + 4]
    m = both_halves(mv)
    first[2].wait()

    def proj_at(p, v):
        r = (p * 32 + v) * 8
        return proj_s[r : r + 8, :]

    base = regroup(tiles_of(proj_at, m))
    lane16 = iota((16, 128), 1)
    keep = [jnp.where((lane16 >> 4) == r8, 1.0, 0.0).astype(BF16) for r8 in range(8)]
    for tx in range(4):
        for tz in range(4):
            h, l = split(jnp.concatenate([base[tx][0][tz], base[tx][1][tz]], axis=0))
            for r8 in range(8):
                r = tx * 128 + r8 * 16
                tp_h[r : r + 16, tz * 128 : tz * 128 + 128] = h * keep[r8]
                tp_l[r : r + 16, tz * 128 : tz * 128 + 128] = l * keep[r8]
    load[0].wait()
    load[1].wait()
    o = dot3(wzh[...], wzl[...], tp_h[...], tp_l[...], NT)
    for t in range(16):
        for ri in range(2):
            for tx in range(4):
                r = t * 4 + ri * 2
                s1[t, ri, 2 * tx : 2 * tx + 2, :] = o[r : r + 2, tx * 128 : tx * 128 + 128]
    pl.semaphore_wait(barrier, len(peers))
    for d in z_order():
        t, dev = z_peer(d)
        send(s1.at[t], r1.at[z], 0, dev)
    r1[pl.ds(z, 1)] = s1[pl.ds(z, 1)]

    for d in (2, 1, 3):
        th = (zh + d) % 4
        dev = (th * NU + u, zl)
        tz_id = th * 4 + zl
        for j in range(2):
            send(spec.at[tz_id + 16 * j], sp.at[zh, j], 4, dev)

        @pl.when(tz_id == 0)
        def _():
            send(spec.at[tz_id + 32], sp.at[zh, 2], 5, dev)

    for e, f in halo:
        dev = near_peer(e, f)
        if f == 0:
            send(ms, hp.at[(1 - e) // 2], 6 + (1 - e) // 2, dev)
        elif f == 1:
            send(bl, ha.at[1 - e], 8, dev)
        else:
            send(bf, hb.at[1 - e], 9, dev)

    for i in (2, 3):
        load[i].wait()
    done(rcv, 0, s1.at[pl.ds(0, 15)])

    zero = jnp.zeros((8, 128), F32)
    whole = low_forward(lambda t, ri: r1[t, ri])
    part = low_forward(lambda t, ri: zero if ri else r1[t, 0])
    y = y_forward(whole, part, lambda k: fh[k], lambda k: fl[k], off)
    for t in range(32):
        s2[t] = y[8 * t : 8 * t + 8]
    for d in u_order():
        t, dev = u_peer(d)
        send(s2.at[t], r2.at[u], 1, dev)
    r2[pl.ds(u, 1)] = s2[pl.ds(u, 1)]

    for i in range(4, 15):
        load[i].wait()
    for c in own:
        c.wait()
    done(rcv, 4, sp.at[pl.ds(0, 3), pl.ds(0, 2)])

    @pl.when(z == 0)
    def _():
        done(rcv, 5, sp.at[pl.ds(0, 3), 0])

    packed = jnp.where(z == 0, 2, 0)
    for zq in range(4):
        for alt in range(2):
            src = (packed if (zq >= 2) != (alt == 1) else 0, 1)
            for k0 in range(4):
                for pos in range(4):
                    k2 = POS_OF_K2.index(pos)
                    for j in range(2):
                        r = k0 * 8 + pos * 2 + j
                        bm[zq, alt, r : r + 1, :] = sp[
                            zq, src[j], k0 : k0 + 1, k2 * 128 : k2 * 128 + 128
                        ]
    sm = spread_spectrum(lambda zq, alt: bm[zq, alt], pick[...])

    done(rcv, 1, s2.at[pl.ds(0, 31)])

    def rows8(ref):
        return lambda i: ref[8 * i : 8 * i + 8, :]

    xh, xl = split(x_input(lambda t: r2[t], rows8(t1c), rows8(t1s)))
    q = dot3(gh[...], gl[...], xh, xl, NN)
    ws = []
    for k1 in range(32):
        a = slice(8 * k1, 8 * k1 + 8)
        c1, c2 = coefficients(sm[a, :128], sm[a, 128:], off, off_u)
        ws.append(x_middle(q[a], k1, t2c[a, :], t2s[a, :], c1, c2))
    xh, xl = split(jnp.concatenate(ws, axis=0))
    o = dot3(gth[...], gtl[...], xh, xl, NN)
    for t in range(32):
        a = slice(8 * t, 8 * t + 8)
        s3[t] = twist(o[a], t1c[a, :], -t1s[a, :])
    for d in u_order():
        t, dev = u_peer(d)
        send(s3.at[t], r3.at[u], 2, dev)
    r3[pl.ds(u, 1)] = s3[pl.ds(u, 1)]
    done(rcv, 2, s3.at[pl.ds(0, 31)])

    v = jnp.concatenate([r3[t] for t in range(32)], axis=0)
    first_part, second_part = y_backward(v, lambda k: fh[k], lambda k: fl[k], off)
    blocks = merge_planes(first_part, second_part, off)
    for t in range(16):
        for ri in range(2):
            s4[t, ri] = blocks[t][ri]
    for d in z_order():
        t, dev = z_peer(d)
        send(s4.at[t], r4.at[z], 3, dev)
    r4[pl.ds(z, 1)] = s4[pl.ds(z, 1)]

    first[3].wait()
    first[4].wait()
    for k in range(6):
        half = nbr_s[4 * k : 4 * k + 4, :]
        nd[k, 0:4, :] = half
        nd[k, 4:8, :] = half
    done(rcv, 6, hp.at[0])
    done(rcv, 7, hp.at[0])
    done(rcv, 8, ha)
    done(rcv, 9, hb)

    def plane(d, i):
        a = slice(8 * i, 8 * i + 8)
        return ms[a, :] if d == 1 else hp[d // 2, a, :]

    low = iota((8, 128), 0) < 4

    def edge(ref):
        def get(d, i):
            pair = ref[d, 2 * i : 2 * i + 2, :]
            return jnp.where(
                low,
                jnp.broadcast_to(pair[0:1], (8, 128)),
                jnp.broadcast_to(pair[1:2], (8, 128)),
            )

        return get

    def near_at(k, p, i):
        r = ((k * 8 + p) * 4 + i) * 8
        return near_s[r : r + 8, :]

    near_sum = near_of(plane, edge(ha), edge(hb), lambda k: nd[k], near_at)

    done(rcv, 3, s4.at[pl.ds(0, 15)])

    rt = jnp.concatenate([r4[t, ri] for t in range(16) for ri in range(2)], axis=0).T
    th, tl = split(rt)
    xs_h, xs_l = [], []
    for tx in range(4):
        mk = jnp.where(((lane16 >> 1) & 3) == tx, 1.0, 0.0).astype(BF16)
        mk = jnp.concatenate([jnp.concatenate([mk, mk], axis=1)] * 8, axis=0)
        xs_h.append(th * mk)
        xs_l.append(tl * mk)
    o = dot3(jnp.concatenate(xs_h, axis=0), jnp.concatenate(xs_l, axis=0), wxh[...], wxl[...], NN)

    def o_at(tx, r8, a, tz):
        r = tx * 128 + r8 * 16 + a * 8
        return o[r : r + 8, tz * 128 : tz * 128 + 128]

    far = far_of(proj_at, ungroup(z_backward_fold(o_at)))
    row = iota((8, 128), 0)
    both = cc[...]
    for i in range(4):
        a, b = far[2 * i] + near_sum[2 * i], far[2 * i + 1] + near_sum[2 * i + 1]
        tot = jnp.where(low, a + sub4(a), b + sub4(b))
        out[8 * i : 8 * i + 8, :] = jnp.where(2 * i + (row >> 2) < both, tot, 0.0)

    done(snd, 0, s1.at[pl.ds(0, 15)])
    done(snd, 1, s2.at[pl.ds(0, 31)])
    done(snd, 2, s3.at[pl.ds(0, 31)])
    done(snd, 3, s4.at[pl.ds(0, 15)])
    done(snd, 4, sp.at[pl.ds(0, 3), pl.ds(0, 2)])

    for d in (2, 1, 3):

        @pl.when(((zh + d) % 4) * 4 + zl == 0)
        def _():
            done(snd, 5, sp.at[0, 0])

    done(snd, 6, ms)
    done(snd, 7, ms)
    done(snd, 8, ha)
    done(snd, 9, hb)


def per_device(charges, counts, projection, near_blocks, neighbours, spectrum):
    tabs = [jnp.asarray(t) for t in tables()]
    ins = [
        charges.reshape(32, 128),
        counts.reshape(4, 128),
        projection.reshape(2048, 128),
        near_blocks.reshape(1536, 128),
        neighbours.reshape(24, 128),
        jnp.transpose(spectrum, (1, 2, 0)),
    ]
    vm = pltpu.VMEM
    scratch = [vm(t.shape, t.dtype) for t in tabs]
    scratch += [vm(a.shape, a.dtype) for a in ins[:5]]
    scratch += [
        vm((4, 3, 4, 512), F32),
        vm((4, 2, 32, 128), F32),
        vm((6, 8, 128), jnp.int32),
        vm((512, 512), BF16),
        vm((512, 512), BF16),
    ]
    scratch += [vm((16, 2, 8, 128), F32)] * 2 + [vm((32, 8, 128), F32)] * 4
    scratch += [vm((16, 2, 8, 128), F32)] * 2
    scratch += [
        vm((32, 128), F32),
        vm((8, 128), F32),
        vm((8, 128), F32),
        vm((2, 32, 128), F32),
        vm((3, 8, 128), F32),
        vm((3, 8, 128), F32),
        vm((8, 128), jnp.int32),
    ]
    dma = pltpu.SemaphoreType.DMA
    scratch += [dma((5,)), dma((15,)), dma((3,)), dma((10,)), dma((10,))]
    res = pl.pallas_call(
        body,
        out_shape=jax.ShapeDtypeStruct((32, 128), F32),
        in_specs=[pl.BlockSpec(memory_space=pl.ANY)] * (6 + len(tabs)),
        out_specs=pl.BlockSpec(memory_space=pltpu.VMEM),
        scratch_shapes=scratch,
        compiler_params=pltpu.CompilerParams(collective_id=0, has_side_effects=True),
        name="potential",
    )(*ins, *tabs)
    return res.reshape(8, 1, 512)


def solution(mesh):
    in_specs = (
        P(None, "slab", "cell"),
        P("slab", "cell"),
        P(None, None, "slab", "cell"),
        P(None, None, None, "slab", "cell"),
        P(None, "slab", "cell"),
        P(None, None, "slab"),
    )
    return jax.shard_map(
        per_device, mesh=mesh, in_specs=in_specs, out_specs=P(None, "slab", "cell"), check_vma=False
    )
```

```python
import functools

import jax
import jax.numpy as jnp
import numpy as np
from jax import lax
from jax.experimental import pallas as pl
from jax.experimental.pallas import tpu as pltpu
from jax.sharding import PartitionSpec as P

F32 = jnp.float32
BF16 = jnp.bfloat16
NZ_RING = 16
NU = 32
SCALE = 1.0 / 16777216.0
POS_OF_K2 = (0, 2, 1, 3)


def split_np(table):
    hi = table.astype(np.float32).astype(jnp.bfloat16)
    lo = (table - hi.astype(np.float64)).astype(jnp.bfloat16)
    return hi, lo


def cis(num, den):
    ang = 2.0 * np.pi * (num % den) / den
    return np.cos(ang), np.sin(ang)


def slot_freq(z, j):
    return z + 16 * j


def z_table():
    tab = np.zeros((16, 2, 2, 4, 8, 16))
    zc = np.arange(16)
    for z in range(16):
        for j in range(2):
            for tz in range(4):
                gz = zc * 4 + tz
                if z == 0 and j == 0:
                    re, im = np.ones(16), 1.0 - 2.0 * (gz % 2)
                else:
                    c, s = cis(slot_freq(z, j) * gz, 64)
                    re, im = c, -s
                tab[z, 0, j, tz] = re
                tab[z, 1, j, tz] = im
    return tab.reshape(64, 512)


def z_table_wide():
    tab = z_table().reshape(16, 2, 1, 2, 512)
    return np.broadcast_to(tab, (16, 2, 4, 2, 512)).reshape(256, 512)


def y_table():
    r8, ty, l = np.meshgrid(np.arange(8), np.arange(4), np.arange(4), indexing="ij")
    low = (l * 32 + r8 * 4 + ty).reshape(-1)
    k0, u, zq = np.meshgrid(np.arange(4), np.arange(32), np.arange(4), indexing="ij")
    ky = zq * 128 + u * 4 + k0
    c, s = cis(ky[..., None] * low, 512)
    tab = np.zeros((4, 32, 2, 4, 2, 128))
    tab[:, :, 0, :, 0] = c
    tab[:, :, 0, :, 1] = s
    tab[:, :, 1, :, 0] = -s
    tab[:, :, 1, :, 1] = c
    return tab.reshape(4, 256, 256)


def x_table():
    c, s = cis(np.arange(32)[:, None] * np.arange(32)[None, :], 32)
    tab = np.zeros((32, 2, 4, 32, 2, 4))
    for q in range(4):
        tab[:, 0, q, :, 0, q] = c
        tab[:, 0, q, :, 1, q] = s
        tab[:, 1, q, :, 0, q] = -s
        tab[:, 1, q, :, 1, q] = c
    return tab.reshape(256, 256)


def lane_parts():
    lane = np.arange(128)
    return lane // 32, (lane // 8) % 4, (lane // 2) % 4, lane % 2


def twist_table(u_or_k1, second):
    k0, kx0, tx, _ = lane_parts()
    row = np.arange(32)[:, None]
    num = tx[None] * (kx0[None] + 4 * row) if second else 4 * row * kx0[None]
    c, s = cis(num, 512)
    cc = np.zeros((32, 2, 4, 128))
    ss = np.zeros((32, 2, 4, 128))
    cc[:] = c[:, None, None, :]
    ss[:, 0] = s[:, None, :]
    ss[:, 1] = -s[:, None, :]
    return cc.reshape(256, 128).astype(np.float32), ss.reshape(256, 128).astype(np.float32)


def pick_table():
    tab = np.zeros((32, 2, 4, 4, 128))
    for k1 in range(32):
        for q in range(4):
            tab[k1, :, q, q, 4 * k1 : 4 * k1 + 4] = 1.0
    return tab.reshape(256, 512)


@functools.cache
def tables():
    out = []
    zt = z_table()
    out += list(split_np(zt))
    out += list(split_np(y_table()))
    g = x_table()
    out += list(split_np(g))
    out += list(split_np(g.T))
    out += list(twist_table(None, False))
    out += list(twist_table(None, True))
    out.append(pick_table().astype(jnp.bfloat16))
    out += list(split_np(z_table_wide()))
    return tuple(np.asarray(t) for t in out)


def roll(x, shift, axis):
    if axis == 1 and x.shape[1] > 128:
        return jnp.concatenate([roll(x[:, i : i + 128], shift, 1) for i in range(0, x.shape[1], 128)], axis=1)
    return pltpu.roll(x, shift % x.shape[axis], axis)


def sub4(x):
    return roll(x, 4, 0)


def iota(shape, dim):
    return lax.broadcasted_iota(jnp.int32, shape, dim)


def split(x):
    hi = x.astype(BF16)
    return hi, (x - hi.astype(F32)).astype(BF16)


NN = (((1,), (0,)), ((), ()))
NT = (((1,), (1,)), ((), ()))


def dot(a, b, dims):
    return lax.dot_general(a, b, dims, preferred_element_type=F32)


def dot3(ah, al, bh, bl, dims):
    return dot(ah, bh, dims) + (dot(al, bh, dims) + dot(ah, bl, dims))


def four_point(parts, sign):
    (ar, ai), (br, bi), (cr, ci), (dr, di) = parts
    pr, pi, mr, mi = ar + cr, ai + ci, ar - cr, ai - ci
    qr, qi, nr, ni = br + dr, bi + di, br - dr, bi - di
    if sign < 0:
        return [(pr + qr, pi + qi), (mr + ni, mi - nr), (pr - qr, pi - qi), (mr - ni, mi + nr)]
    return [(pr + qr, pi + qi), (mr - ni, mi + nr), (pr - qr, pi - qi), (mr + ni, mi - nr)]


def lane_partner(x, stride, bit):
    return jnp.where(bit == 0, roll(x, -stride, 1), roll(x, stride, 1))


def swap_signed(x, ri, sign):
    r = sub4(x)
    return jnp.where(ri == 0, -r, r) if sign > 0 else jnp.where(ri == 0, r, -r)


def lane_dft4(x, sign):
    lane = iota(x.shape, 1)
    ri = (iota(x.shape, 0) >> 2) & 1
    b1, b0 = (lane >> 2) & 1, (lane >> 1) & 1
    if sign < 0:
        a = lane_partner(x, 4, b1)
        x = jnp.where(b1 == 0, x + a, a - x)
        x = jnp.where((b1 == 1) & (b0 == 1), swap_signed(x, ri, -1), x)
        c = lane_partner(x, 2, b0)
        return jnp.where(b0 == 0, x + c, c - x)
    c = lane_partner(x, 2, b0)
    x = jnp.where(b0 == 0, x + c, c - x)
    x = jnp.where((b1 == 1) & (b0 == 1), swap_signed(x, ri, 1), x)
    a = lane_partner(x, 4, b1)
    return jnp.where(b1 == 0, x + a, a - x)


def masked_charges(ch, cnt):
    row = iota((8, 128), 0)
    return [jnp.where(2 * i + (row >> 2) < cnt, ch(i), 0.0) for i in range(4)]


def both_halves(mv):
    row = iota((8, 128), 0)
    out = []
    for v in mv:
        r = sub4(v)
        out += [jnp.where(row < 4, v, r), jnp.where(row < 4, r, v)]
    return out


def tiles_of(proj, m):
    out = []
    for v in range(32):
        acc = proj(0, v) * m[0]
        for p in range(1, 8):
            acc = acc + proj(p, v) * m[p]
        out.append(acc)
    return out


def regroup(tile):
    low = iota((8, 128), 0) < 4
    base = [[[None] * 4 for _ in range(2)] for _ in range(4)]
    for tx in range(4):
        for a in range(2):
            for h in range(2):
                v0, v1 = tile[tx * 8 + 4 * a + h], tile[tx * 8 + 4 * a + 2 + h]
                base[tx][a][2 * h] = jnp.where(low, v0, sub4(v1))
                base[tx][a][2 * h + 1] = jnp.where(low, sub4(v0), v1)
    return base


def ungroup(e):
    low = iota((8, 128), 0) < 4
    out = [None] * 32
    for tx in range(4):
        for a in range(2):
            for h in range(2):
                p, q = e[tx][a][2 * h], e[tx][a][2 * h + 1]
                out[tx * 8 + 4 * a + h] = jnp.where(low, p, sub4(q))
                out[tx * 8 + 4 * a + 2 + h] = jnp.where(low, sub4(p), q)
    return out


def y_fixup(whole, part, k0, off):
    lane, row = iota(whole.shape, 1), iota(whole.shape, 0)
    zq, ri, u = lane & 3, (lane >> 2) & 1, lane >> 3
    rest = whole - part
    swapped = jnp.where(ri == 0, roll(rest, -4, 1), -roll(rest, 4, 1))
    alone = (u == 0) & ((zq & 1) == 0) if k0 == 0 else (lane < 0)
    special = ((row & 1) + off == 0) & jnp.logical_not(alone)
    return jnp.where(special, jnp.where(zq < 2, part, swapped), whole)


def y_forward(whole, part, fh, fl, off):
    rows = []
    for k0 in range(4):
        x = jnp.concatenate(
            [
                jnp.concatenate([jnp.concatenate(y[k0], axis=0) for y in pair], axis=1)
                for pair in (whole, part)
            ],
            axis=0,
        )
        xh, xl = split(x)
        o = dot3(xh, xl, fh(k0), fl(k0), NT)
        rows.append(y_fixup(o[:32], o[32:], k0, off))
    return jnp.concatenate(rows, axis=0).T


def y_backward(v, fh, fl, off):
    vt = v.T
    first, second = ([], []), ([], [])
    for k0 in range(4):
        a = vt[k0 * 32 : k0 * 32 + 32]
        lane, row = iota(a.shape, 1), iota(a.shape, 0)
        zq, ri, u = lane & 3, (lane >> 2) & 1, lane >> 3
        special = (row & 1) + off == 0
        alone = (u == 0) & ((zq & 1) == 0) if k0 == 0 else (lane < 0)
        va = jnp.where(special & (zq >= 2) & jnp.logical_not(alone), 0.0, a)
        vb = jnp.where(zq >= 2, a, 0.0)
        if k0 == 0:
            vb = jnp.where(alone, jnp.where(ri == 0, roll(a, -4, 1), -roll(a, 4, 1)), vb)
        xh, xl = split(jnp.concatenate([va, vb], axis=0))
        o = dot3(xh, xl, fh(k0), fl(k0), NN)
        for half, pair in enumerate((first, second)):
            for ri_part in range(2):
                pair[ri_part].append(
                    [
                        o[32 * half + 8 * q : 32 * half + 8 * q + 8, 128 * ri_part : 128 * ri_part + 128]
                        for q in range(4)
                    ]
                )
    return first, second


def low_forward(r1):
    inner = [
        four_point([(r1(zh * 4 + zl, 0), r1(zh * 4 + zl, 1)) for zl in range(4)], -1)
        for zh in range(4)
    ]
    yr, yi = [], []
    for k0 in range(4):
        o = four_point([inner[zh][k0] for zh in range(4)], -1)
        yr.append([p[0] for p in o])
        yi.append([p[1] for p in o])
    return yr, yi


def low_backward(y):
    inner = [four_point(list(zip(y[0][k0], y[1][k0])), 1) for k0 in range(4)]
    return [four_point([inner[k0][zh] for k0 in range(4)], 1) for zh in range(4)]


def merge_planes(first, second, off):
    special = (iota((8, 128), 0) & 1) + off == 0
    a, b = low_backward(first), low_backward(second)
    return [
        (a[z // 4][z % 4][0], jnp.where(special, b[z // 4][z % 4][0], a[z // 4][z % 4][1]))
        for z in range(16)
    ]


def twist(x, c, s):
    return x * c + sub4(x) * s


def x_input(r2, tc, ts):
    lane, row = iota((8, 128), 1), iota((8, 128), 0)
    kx0 = (lane >> 3) & 3
    main, conj = [], []
    for u in range(32):
        v = r2(u)
        w = jnp.where(kx0 == 1, roll(v, -16, 1), jnp.where(kx0 == 3, roll(v, 16, 1), v))
        w = jnp.where(row < 4, w, -w)
        main.append(twist(v, tc(u), ts(u)))
        conj.append(twist(w, tc(u), ts(u)))
    return jnp.concatenate(
        [jnp.concatenate(main, axis=0), jnp.concatenate(conj, axis=0)], axis=1
    )


def x_middle(q, k1, tc, ts, c1, c2):
    a = lane_dft4(twist(q[:, :128], tc, ts), -1)
    b = lane_dft4(twist(q[:, 128:], tc, ts), -1)
    return twist(lane_dft4(a * c1 + b * c2, 1), tc, -ts)


def coefficients(sm, sa, off, off_u):
    lane, row = iota((8, 128), 1), iota((8, 128), 0)
    zq = row & 3
    special = (lane >> 5) + (lane & 1) + (zq & 1) + off + off_u == 0
    c1 = jnp.where(special, 0.5 * SCALE * (sm + sa), 2.0 * SCALE * sm)
    half = 0.5 * SCALE * (sm - sa)
    c2 = jnp.where(special, jnp.where(zq < 2, half, -half), 0.0)
    return c1, c2


def spread_spectrum(rows, pick):
    lane = iota((8, 128), 1)
    keep = [(lane & 3) == kx0 for kx0 in range(4)]
    cols = []
    for zq in range(4):
        parts = []
        for alt in range(2):
            b = rows(zq, alt)
            for k0 in range(4):
                for kx0 in range(4):
                    parts.append(jnp.where(keep[kx0], b[8 * k0 : 8 * k0 + 8], 0.0))
        cols.append(jnp.concatenate(parts, axis=0))
    m = jnp.concatenate(cols, axis=1)
    h, l = split(m)
    return dot(pick, h, NT) + dot(pick, l, NT)


def z_backward_fold(o):
    lane = iota((8, 128), 1)
    e = [[[None] * 4 for _ in range(2)] for _ in range(4)]
    for tx in range(4):
        for a in range(2):
            for tz in range(4):
                acc = o(tx, 0, a, tz)
                for r8 in range(1, 8):
                    acc = jnp.where((lane >> 4) == r8, o(tx, r8, a, tz), acc)
                e[tx][a][tz] = acc
    return e


def far_of(proj, pot):
    out = []
    for p in range(8):
        acc = proj(p, 0) * pot[0]
        for v in range(1, 32):
            acc = acc + proj(p, v) * pot[v]
        out.append(acc)
    return out


def near_of(plane, above, below, codes, near):
    lane, row = iota((8, 128), 1), iota((8, 128), 0)
    l, zc = row & 3, lane & 15
    code = [codes(k) for k in range(6)]
    picked = [[jnp.zeros((8, 128), F32)] * 4 for _ in range(6)]
    for d in range(3):
        for i in range(4):
            v = plane(d, i)
            up = roll(v, -16, 1)
            nxt = jnp.where(l == 3, roll(below(d, i), -16, 1), roll(up, -1, 0))
            after = jnp.where(lane >= 112, nxt, up)
            dn = roll(v, 16, 1)
            prv = jnp.where(l == 0, roll(above(d, i), 16, 1), roll(dn, 1, 0))
            before = jnp.where(lane < 16, prv, dn)
            for e, w in enumerate((before, v, after)):
                plus = jnp.where(zc == 15, roll(w, 15, 1), roll(w, -1, 1))
                minus = jnp.where(zc == 0, roll(w, -15, 1), roll(w, 1, 1))
                for f, x in enumerate((minus, w, plus)):
                    for k in range(6):
                        if k == 0 and (d, e, f) != (1, 1, 1):
                            continue
                        if k > 0 and (d, e, f) == (1, 1, 1):
                            continue
                        picked[k][i] = (
                            x if k == 0 else jnp.where(code[k] == 9 * d + 3 * e + f, x, picked[k][i])
                        )
    out = []
    for p in range(8):
        acc = None
        for k in range(6):
            for i in range(4):
                t = near(k, p, i) * picked[k][i]
                acc = t if acc is None else acc + t
        out.append(acc)
    return out


def z_order():
    out = []
    for step in range(8, 0, -1):
        out += [step] if step == 8 else [step, 16 - step]
    return out


def u_order():
    far = (0, 1, 2, 1)
    out = [(x, y, c) for x in range(4) for y in range(4) for c in range(2)]
    out.remove((0, 0, 0))
    return sorted(out, key=lambda t: (-far[t[0]] - far[t[1]], t))


def body(
    ch,
    cnt,
    proj,
    near,
    nbr,
    spec,
    *rest,
):
    tab_in, (out,), scr = rest[:15], rest[15:16], rest[16:]
    tab = scr[:15]
    (ch_s, cnt_s, proj_s, near_s, nbr_s) = scr[15:20]
    (sp, bm, nd, tp_h, tp_l) = scr[20:25]
    (s1, r1, s2, r2, s3, r3, s4, r4) = scr[25:33]
    (ms, bf, bl, hp, ha, hb, cc, rb, rs) = scr[33:42]
    (in_sem, tab_sem, loc_sem, snd, rcv, rsem) = scr[42:]
    (wzh, wzl, fh, fl, gh, gl, gth, gtl, t1c, t1s, t2c, t2s, pick, wxh, wxl) = tab

    slab, zl = lax.axis_index("slab"), lax.axis_index("cell")
    slabs = lax.axis_size("slab")
    zh, u = slab // NU, slab % NU
    z = zh * 4 + zl
    off = z
    off_u = u

    def z_dev(t):
        return ((t // 4) * NU + u, t % 4)

    def z_peer(d):
        t = (z + d + 16) % 16
        return t, z_dev(t)

    def u_peer(d):
        t = ((u // 8 + d[0]) % 4) * 8 + ((u // 2 % 4 + d[1]) % 4) * 2 + (u + d[2]) % 2
        return t, (zh * NU + t, zl)

    def near_peer(e, f):
        return ((slab + slabs + e) % slabs, (zl + 4 + f) % 4)

    halo = [(e, f) for e in (-1, 0, 1) for f in (-1, 0, 1) if (e, f) != (0, 0)]

    first = [
        pltpu.make_async_copy(a, b, in_sem.at[i])
        for i, (a, b) in enumerate(
            ((ch, ch_s), (cnt, cnt_s), (proj, proj_s), (nbr, nbr_s), (near, near_s))
        )
    ]
    load = [pltpu.make_async_copy(a, b, tab_sem.at[i]) for i, (a, b) in enumerate(zip(tab_in, tab))]
    for c in first[:3] + load[:2]:
        c.start()

    barrier = pltpu.get_barrier_semaphore()
    peers = [z_peer(d)[1] for d in (12, 4, 13, 3, 14, 2, 15, 1)] + [u_peer(d)[1] for d in u_order()]
    for p in peers:
        pl.semaphore_signal(barrier, inc=1, device_id=p, device_id_type=pl.DeviceIdType.MESH)
    for c in load[2:] + first[3:]:
        c.start()
    own = [
        pltpu.make_async_copy(spec.at[z + 16 * j], sp.at[zh, j], loc_sem.at[j]) for j in range(3)
    ]
    for c in own:
        c.start()

    def send(src, dst, i, dev, arrival=None):
        pltpu.make_async_remote_copy(
            src_ref=src,
            dst_ref=dst,
            send_sem=snd.at[i],
            recv_sem=rcv.at[i] if arrival is None else arrival,
            device_id=dev,
            device_id_type=pl.DeviceIdType.MESH,
        ).start()

    def done(sem, i, ref):
        pltpu.make_async_copy(ref, ref, sem.at[i]).wait()

    first[0].wait()
    first[1].wait()
    half = cnt_s[...]
    cc[0:4, :] = half
    cc[4:8, :] = half
    mv = masked_charges(lambda i: ch_s[8 * i : 8 * i + 8, :], cc[...])
    for i in range(4):
        ms[8 * i : 8 * i + 8, :] = mv[i]
        for h in range(2):
            bf[2 * i + h : 2 * i + h + 1, :] = mv[i][4 * h : 4 * h + 1]
            bl[2 * i + h : 2 * i + h + 1, :] = mv[i][4 * h + 3 : 4 * h + 4]
    m = both_halves(mv)
    first[2].wait()

    def proj_at(p, v):
        r = (p * 32 + v) * 8
        return proj_s[r : r + 8, :]

    base = regroup(tiles_of(proj_at, m))
    lane16 = iota((16, 128), 1)
    keep = [jnp.where((lane16 >> 4) == r8, 1.0, 0.0).astype(BF16) for r8 in range(8)]
    for tx in range(4):
        for tz in range(4):
            h, l = split(jnp.concatenate([base[tx][0][tz], base[tx][1][tz]], axis=0))
            for r8 in range(8):
                r = tx * 128 + r8 * 16
                tp_h[r : r + 16, tz * 128 : tz * 128 + 128] = h * keep[r8]
                tp_l[r : r + 16, tz * 128 : tz * 128 + 128] = l * keep[r8]
    load[0].wait()
    load[1].wait()
    o = dot3(wzh[...], wzl[...], tp_h[...], tp_l[...], NT)
    for t in range(16):
        for ri in range(2):
            for tx in range(4):
                r = t * 4 + ri * 2
                s1[t, ri, 2 * tx : 2 * tx + 2, :] = o[r : r + 2, tx * 128 : tx * 128 + 128]
    pl.semaphore_wait(barrier, len(peers))

    core = u % 2
    opp_in, opp_out = (z + 12 + 8 * core) % 16, (z + 4 + 8 * core) % 16
    relays = []
    for m in (3, 2, 1):
        for side, sgn in ((0, 1), (1, -1)):
            relays.append((side * 3 + m - 1, (z + 16 + sgn * (4 + m)) % 16, z_peer(4 * sgn)[1], z_peer(-4 * sgn)[0], z_peer(m * sgn)[1]))
    opp = (6, (z + 8) % 16, z_dev(opp_out), opp_in, z_dev(opp_out))
    relays = [opp] + relays
    for slot, t, dev, _, _ in relays:
        send(s1.at[t], rb.at[slot], 0, dev, rsem.at[slot])
    for d in (4, 12, 3, 13, 2, 14, 1, 15):
        t, dev = z_peer(d)
        send(s1.at[t], r1.at[z], 0, dev)
    r1[pl.ds(z, 1)] = s1[pl.ds(z, 1)]

    far_id = (z + 8) % 16
    for j in range(2):
        send(spec.at[far_id + 16 * j], rs.at[j], 4, z_dev(opp_out), rsem.at[7 + j])

    @pl.when(far_id == 0)
    def _():
        send(spec.at[far_id + 32], rs.at[2], 5, z_dev(opp_out), rsem.at[9])

    for slot, _, _, src, dev in relays:
        done(rsem, slot, rb.at[slot])
        send(rb.at[slot], r1.at[src], 10, dev, rcv.at[0])

    for d in (4, 12):
        t, dev = z_peer(d)
        for j in range(2):
            send(spec.at[t + 16 * j], sp.at[zh, j], 4, dev)

        @pl.when(t == 0)
        def _():
            send(spec.at[t + 32], sp.at[zh, 2], 5, dev)

    for j in range(2):
        done(rsem, 7 + j, rs.at[j])
        send(rs.at[j], sp.at[opp_in // 4, j], 11, z_dev(opp_out), rcv.at[4])

    @pl.when(opp_out == 0)
    def _():
        done(rsem, 9, rs.at[2])
        send(rs.at[2], sp.at[opp_in // 4, 2], 12, z_dev(opp_out), rcv.at[5])

    for i in (2, 3):
        load[i].wait()
    done(rcv, 0, s1.at[pl.ds(0, 15)])

    zero = jnp.zeros((8, 128), F32)
    whole = low_forward(lambda t, ri: r1[t, ri])
    part = low_forward(lambda t, ri: zero if ri else r1[t, 0])
    y = y_forward(whole, part, lambda k: fh[k], lambda k: fl[k], off)
    for t in range(32):
        s2[t] = y[8 * t : 8 * t + 8]
    for d in u_order():
        t, dev = u_peer(d)
        send(s2.at[t], r2.at[u], 1, dev)
    r2[pl.ds(u, 1)] = s2[pl.ds(u, 1)]

    for i in range(4, 15):
        load[i].wait()
    for c in own:
        c.wait()
    done(rcv, 4, sp.at[pl.ds(0, 3), pl.ds(0, 2)])

    @pl.when(z == 0)
    def _():
        done(rcv, 5, sp.at[pl.ds(0, 3), 0])

    packed = jnp.where(z == 0, 2, 0)
    for zq in range(4):
        for alt in range(2):
            src = (packed if (zq >= 2) != (alt == 1) else 0, 1)
            for k0 in range(4):
                for pos in range(4):
                    k2 = POS_OF_K2.index(pos)
                    for j in range(2):
                        r = k0 * 8 + pos * 2 + j
                        bm[zq, alt, r : r + 1, :] = sp[
                            zq, src[j], k0 : k0 + 1, k2 * 128 : k2 * 128 + 128
                        ]
    sm = spread_spectrum(lambda zq, alt: bm[zq, alt], pick[...])

    done(rcv, 1, s2.at[pl.ds(0, 31)])

    def rows8(ref):
        return lambda i: ref[8 * i : 8 * i + 8, :]

    xh, xl = split(x_input(lambda t: r2[t], rows8(t1c), rows8(t1s)))
    q = dot3(gh[...], gl[...], xh, xl, NN)
    ws = []
    for k1 in range(32):
        a = slice(8 * k1, 8 * k1 + 8)
        c1, c2 = coefficients(sm[a, :128], sm[a, 128:], off, off_u)
        ws.append(x_middle(q[a], k1, t2c[a, :], t2s[a, :], c1, c2))
    xh, xl = split(jnp.concatenate(ws, axis=0))
    o = dot3(gth[...], gtl[...], xh, xl, NN)
    for t in range(32):
        a = slice(8 * t, 8 * t + 8)
        s3[t] = twist(o[a], t1c[a, :], -t1s[a, :])
    for d in u_order():
        t, dev = u_peer(d)
        send(s3.at[t], r3.at[u], 2, dev)
    r3[pl.ds(u, 1)] = s3[pl.ds(u, 1)]

    for e, f in halo:
        dev = near_peer(e, f)
        if f == 0:
            send(ms, hp.at[(1 - e) // 2], 6 + (1 - e) // 2, dev)
        elif f == 1:
            send(bl, ha.at[1 - e], 8, dev)
        else:
            send(bf, hb.at[1 - e], 9, dev)
    done(rcv, 2, s3.at[pl.ds(0, 31)])

    v = jnp.concatenate([r3[t] for t in range(32)], axis=0)
    first_part, second_part = y_backward(v, lambda k: fh[k], lambda k: fl[k], off)
    blocks = merge_planes(first_part, second_part, off)
    for t in range(16):
        for ri in range(2):
            s4[t, ri] = blocks[t][ri]
    for d in z_order():
        t, dev = z_peer(d)
        send(s4.at[t], r4.at[z], 3, dev)
    r4[pl.ds(z, 1)] = s4[pl.ds(z, 1)]

    first[3].wait()
    first[4].wait()
    for k in range(6):
        half = nbr_s[4 * k : 4 * k + 4, :]
        nd[k, 0:4, :] = half
        nd[k, 4:8, :] = half
    done(rcv, 6, hp.at[0])
    done(rcv, 7, hp.at[0])
    done(rcv, 8, ha)
    done(rcv, 9, hb)

    def plane(d, i):
        a = slice(8 * i, 8 * i + 8)
        return ms[a, :] if d == 1 else hp[d // 2, a, :]

    low = iota((8, 128), 0) < 4

    def edge(ref):
        def get(d, i):
            pair = ref[d, 2 * i : 2 * i + 2, :]
            return jnp.where(
                low,
                jnp.broadcast_to(pair[0:1], (8, 128)),
                jnp.broadcast_to(pair[1:2], (8, 128)),
            )

        return get

    def near_at(k, p, i):
        r = ((k * 8 + p) * 4 + i) * 8
        return near_s[r : r + 8, :]

    near_sum = near_of(plane, edge(ha), edge(hb), lambda k: nd[k], near_at)

    done(rcv, 3, s4.at[pl.ds(0, 15)])

    rt = jnp.concatenate([r4[t, ri] for t in range(16) for ri in range(2)], axis=0).T
    th, tl = split(rt)
    xs_h, xs_l = [], []
    for tx in range(4):
        mk = jnp.where(((lane16 >> 1) & 3) == tx, 1.0, 0.0).astype(BF16)
        mk = jnp.concatenate([jnp.concatenate([mk, mk], axis=1)] * 8, axis=0)
        xs_h.append(th * mk)
        xs_l.append(tl * mk)
    o = dot3(jnp.concatenate(xs_h, axis=0), jnp.concatenate(xs_l, axis=0), wxh[...], wxl[...], NN)

    def o_at(tx, r8, a, tz):
        r = tx * 128 + r8 * 16 + a * 8
        return o[r : r + 8, tz * 128 : tz * 128 + 128]

    far = far_of(proj_at, ungroup(z_backward_fold(o_at)))
    row = iota((8, 128), 0)
    both = cc[...]
    for i in range(4):
        a, b = far[2 * i] + near_sum[2 * i], far[2 * i + 1] + near_sum[2 * i + 1]
        tot = jnp.where(low, a + sub4(a), b + sub4(b))
        out[8 * i : 8 * i + 8, :] = jnp.where(2 * i + (row >> 2) < both, tot, 0.0)

    done(snd, 0, s1.at[pl.ds(0, 15)])
    done(snd, 1, s2.at[pl.ds(0, 31)])
    done(snd, 2, s3.at[pl.ds(0, 31)])
    done(snd, 3, s4.at[pl.ds(0, 15)])
    done(snd, 4, sp.at[pl.ds(0, 3), pl.ds(0, 2)])

    for t in ((z + 8) % 16, (z + 4) % 16, (z + 12) % 16):

        @pl.when(t == 0)
        def _():
            done(snd, 5, sp.at[0, 0])

    @pl.when(opp_out == 0)
    def _():
        done(snd, 12, sp.at[0, 0])

    done(snd, 10, s1.at[pl.ds(0, 7)])
    done(snd, 11, rs.at[pl.ds(0, 2)])

    done(snd, 6, ms)
    done(snd, 7, ms)
    done(snd, 8, ha)
    done(snd, 9, hb)


def per_device(charges, counts, projection, near_blocks, neighbours, spectrum):
    tabs = [jnp.asarray(t) for t in tables()]
    ins = [
        charges.reshape(32, 128),
        counts.reshape(4, 128),
        projection.reshape(2048, 128),
        near_blocks.reshape(1536, 128),
        neighbours.reshape(24, 128),
        jnp.transpose(spectrum, (1, 2, 0)),
    ]
    vm = pltpu.VMEM
    scratch = [vm(t.shape, t.dtype) for t in tabs]
    scratch += [vm(a.shape, a.dtype) for a in ins[:5]]
    scratch += [
        vm((4, 3, 4, 512), F32),
        vm((4, 2, 32, 128), F32),
        vm((6, 8, 128), jnp.int32),
        vm((512, 512), BF16),
        vm((512, 512), BF16),
    ]
    scratch += [vm((16, 2, 8, 128), F32)] * 2 + [vm((32, 8, 128), F32)] * 4
    scratch += [vm((16, 2, 8, 128), F32)] * 2
    scratch += [
        vm((32, 128), F32),
        vm((8, 128), F32),
        vm((8, 128), F32),
        vm((2, 32, 128), F32),
        vm((3, 8, 128), F32),
        vm((3, 8, 128), F32),
        vm((8, 128), jnp.int32),
        vm((7, 2, 8, 128), F32),
        vm((3, 4, 512), F32),
    ]
    dma = pltpu.SemaphoreType.DMA
    scratch += [dma((5,)), dma((15,)), dma((3,)), dma((13,)), dma((10,)), dma((10,))]
    res = pl.pallas_call(
        body,
        out_shape=jax.ShapeDtypeStruct((32, 128), F32),
        in_specs=[pl.BlockSpec(memory_space=pl.ANY)] * (6 + len(tabs)),
        out_specs=pl.BlockSpec(memory_space=pltpu.VMEM),
        scratch_shapes=scratch,
        compiler_params=pltpu.CompilerParams(collective_id=0, has_side_effects=True),
        name="potential",
    )(*ins, *tabs)
    return res.reshape(8, 1, 512)


def solution(mesh):
    in_specs = (
        P(None, "slab", "cell"),
        P("slab", "cell"),
        P(None, None, "slab", "cell"),
        P(None, None, None, "slab", "cell"),
        P(None, "slab", "cell"),
        P(None, None, "slab"),
    )
    return jax.shard_map(
        per_device, mesh=mesh, in_specs=in_specs, out_specs=P(None, "slab", "cell"), check_vma=False
    )
```

```python
import functools

import jax
import jax.numpy as jnp
import numpy as np
from jax import lax
from jax.experimental import pallas as pl
from jax.experimental.pallas import tpu as pltpu
from jax.sharding import PartitionSpec as P

F32 = jnp.float32
BF16 = jnp.bfloat16
NZ_RING = 16
NU = 32
SCALE = 1.0 / 16777216.0
POS_OF_K2 = (0, 2, 1, 3)


def split_np(table):
    hi = table.astype(np.float32).astype(jnp.bfloat16)
    lo = (table - hi.astype(np.float64)).astype(jnp.bfloat16)
    return hi, lo


def cis(num, den):
    ang = 2.0 * np.pi * (num % den) / den
    return np.cos(ang), np.sin(ang)


def slot_freq(z, j):
    return z + 16 * j


def z_table():
    tab = np.zeros((16, 2, 2, 4, 8, 16))
    zc = np.arange(16)
    for z in range(16):
        for j in range(2):
            for tz in range(4):
                gz = zc * 4 + tz
                if z == 0 and j == 0:
                    re, im = np.ones(16), 1.0 - 2.0 * (gz % 2)
                else:
                    c, s = cis(slot_freq(z, j) * gz, 64)
                    re, im = c, -s
                tab[z, 0, j, tz] = re
                tab[z, 1, j, tz] = im
    return tab.reshape(64, 512)


def z_table_wide():
    tab = z_table().reshape(16, 2, 1, 2, 512)
    return np.broadcast_to(tab, (16, 2, 4, 2, 512)).reshape(256, 512)


def y_table():
    r8, ty, l = np.meshgrid(np.arange(8), np.arange(4), np.arange(4), indexing="ij")
    low = (l * 32 + r8 * 4 + ty).reshape(-1)
    k0, u, zq = np.meshgrid(np.arange(4), np.arange(32), np.arange(4), indexing="ij")
    ky = zq * 128 + u * 4 + k0
    c, s = cis(ky[..., None] * low, 512)
    tab = np.zeros((4, 32, 2, 4, 2, 128))
    tab[:, :, 0, :, 0] = c
    tab[:, :, 0, :, 1] = s
    tab[:, :, 1, :, 0] = -s
    tab[:, :, 1, :, 1] = c
    return tab.reshape(4, 256, 256)


def x_table():
    c, s = cis(np.arange(32)[:, None] * np.arange(32)[None, :], 32)
    tab = np.zeros((32, 2, 4, 32, 2, 4))
    for q in range(4):
        tab[:, 0, q, :, 0, q] = c
        tab[:, 0, q, :, 1, q] = s
        tab[:, 1, q, :, 0, q] = -s
        tab[:, 1, q, :, 1, q] = c
    return tab.reshape(256, 256)


def lane_parts():
    lane = np.arange(128)
    return lane // 32, (lane // 8) % 4, (lane // 2) % 4, lane % 2


def twist_table(u_or_k1, second):
    k0, kx0, tx, _ = lane_parts()
    row = np.arange(32)[:, None]
    num = tx[None] * (kx0[None] + 4 * row) if second else 4 * row * kx0[None]
    c, s = cis(num, 512)
    cc = np.zeros((32, 2, 4, 128))
    ss = np.zeros((32, 2, 4, 128))
    cc[:] = c[:, None, None, :]
    ss[:, 0] = s[:, None, :]
    ss[:, 1] = -s[:, None, :]
    return cc.reshape(256, 128).astype(np.float32), ss.reshape(256, 128).astype(np.float32)


def pick_table():
    tab = np.zeros((32, 2, 4, 4, 128))
    for k1 in range(32):
        for q in range(4):
            tab[k1, :, q, q, 4 * k1 : 4 * k1 + 4] = 1.0
    return tab.reshape(256, 512)


@functools.cache
def tables():
    out = []
    zt = z_table()
    out += list(split_np(zt))
    out += list(split_np(y_table()))
    g = x_table()
    out += list(split_np(g))
    out += list(split_np(g.T))
    out += list(twist_table(None, False))
    out += list(twist_table(None, True))
    out.append(pick_table().astype(jnp.bfloat16))
    out += list(split_np(z_table_wide()))
    return tuple(np.asarray(t) for t in out)


def roll(x, shift, axis):
    if axis == 1 and x.shape[1] > 128:
        return jnp.concatenate([roll(x[:, i : i + 128], shift, 1) for i in range(0, x.shape[1], 128)], axis=1)
    return pltpu.roll(x, shift % x.shape[axis], axis)


def sub4(x):
    return roll(x, 4, 0)


def iota(shape, dim):
    return lax.broadcasted_iota(jnp.int32, shape, dim)


def split(x):
    hi = x.astype(BF16)
    return hi, (x - hi.astype(F32)).astype(BF16)


NN = (((1,), (0,)), ((), ()))
NT = (((1,), (1,)), ((), ()))


def dot(a, b, dims):
    return lax.dot_general(a, b, dims, preferred_element_type=F32)


def dot3(ah, al, bh, bl, dims):
    return dot(ah, bh, dims) + (dot(al, bh, dims) + dot(ah, bl, dims))


def four_point(parts, sign):
    (ar, ai), (br, bi), (cr, ci), (dr, di) = parts
    pr, pi, mr, mi = ar + cr, ai + ci, ar - cr, ai - ci
    qr, qi, nr, ni = br + dr, bi + di, br - dr, bi - di
    if sign < 0:
        return [(pr + qr, pi + qi), (mr + ni, mi - nr), (pr - qr, pi - qi), (mr - ni, mi + nr)]
    return [(pr + qr, pi + qi), (mr - ni, mi + nr), (pr - qr, pi - qi), (mr + ni, mi - nr)]


def lane_partner(x, stride, bit):
    return jnp.where(bit == 0, roll(x, -stride, 1), roll(x, stride, 1))


def swap_signed(x, ri, sign):
    r = sub4(x)
    return jnp.where(ri == 0, -r, r) if sign > 0 else jnp.where(ri == 0, r, -r)


def lane_dft4(x, sign):
    lane = iota(x.shape, 1)
    ri = (iota(x.shape, 0) >> 2) & 1
    b1, b0 = (lane >> 2) & 1, (lane >> 1) & 1
    if sign < 0:
        a = lane_partner(x, 4, b1)
        x = jnp.where(b1 == 0, x + a, a - x)
        x = jnp.where((b1 == 1) & (b0 == 1), swap_signed(x, ri, -1), x)
        c = lane_partner(x, 2, b0)
        return jnp.where(b0 == 0, x + c, c - x)
    c = lane_partner(x, 2, b0)
    x = jnp.where(b0 == 0, x + c, c - x)
    x = jnp.where((b1 == 1) & (b0 == 1), swap_signed(x, ri, 1), x)
    a = lane_partner(x, 4, b1)
    return jnp.where(b1 == 0, x + a, a - x)


def masked_charges(ch, cnt):
    row = iota((8, 128), 0)
    return [jnp.where(2 * i + (row >> 2) < cnt, ch(i), 0.0) for i in range(4)]


def both_halves(mv):
    row = iota((8, 128), 0)
    out = []
    for v in mv:
        r = sub4(v)
        out += [jnp.where(row < 4, v, r), jnp.where(row < 4, r, v)]
    return out


def tiles_of(proj, m):
    out = []
    for v in range(32):
        acc = proj(0, v) * m[0]
        for p in range(1, 8):
            acc = acc + proj(p, v) * m[p]
        out.append(acc)
    return out


def regroup(tile):
    low = iota((8, 128), 0) < 4
    base = [[[None] * 4 for _ in range(2)] for _ in range(4)]
    for tx in range(4):
        for a in range(2):
            for h in range(2):
                v0, v1 = tile[tx * 8 + 4 * a + h], tile[tx * 8 + 4 * a + 2 + h]
                base[tx][a][2 * h] = jnp.where(low, v0, sub4(v1))
                base[tx][a][2 * h + 1] = jnp.where(low, sub4(v0), v1)
    return base


def ungroup(e):
    low = iota((8, 128), 0) < 4
    out = [None] * 32
    for tx in range(4):
        for a in range(2):
            for h in range(2):
                p, q = e[tx][a][2 * h], e[tx][a][2 * h + 1]
                out[tx * 8 + 4 * a + h] = jnp.where(low, p, sub4(q))
                out[tx * 8 + 4 * a + 2 + h] = jnp.where(low, sub4(p), q)
    return out


def y_fixup(whole, part, k0, off):
    lane, row = iota(whole.shape, 1), iota(whole.shape, 0)
    zq, ri, u = lane & 3, (lane >> 2) & 1, lane >> 3
    rest = whole - part
    swapped = jnp.where(ri == 0, roll(rest, -4, 1), -roll(rest, 4, 1))
    alone = (u == 0) & ((zq & 1) == 0) if k0 == 0 else (lane < 0)
    special = ((row & 1) + off == 0) & jnp.logical_not(alone)
    return jnp.where(special, jnp.where(zq < 2, part, swapped), whole)


def y_forward(whole, part, fh, fl, off):
    rows = []
    for k0 in range(4):
        pairs = (whole,) if part is None else (whole, part)
        x = [jnp.concatenate([jnp.concatenate(y[k0], axis=0) for y in pair], axis=1) for pair in pairs]
        xh, xl = split(jnp.concatenate(x, axis=0))
        o = dot3(xh, xl, fh(k0), fl(k0), NT)
        rows.append(o if part is None else y_fixup(o[:32], o[32:], k0, off))
    return jnp.concatenate(rows, axis=0).T


def y_backward(v, fh, fl, off, packed=True):
    vt = v.T
    first, second = ([], []), ([], [])
    for k0 in range(4):
        a = vt[k0 * 32 : k0 * 32 + 32]
        lane, row = iota(a.shape, 1), iota(a.shape, 0)
        zq, ri, u = lane & 3, (lane >> 2) & 1, lane >> 3
        special = (row & 1) + off == 0
        alone = (u == 0) & ((zq & 1) == 0) if k0 == 0 else (lane < 0)
        va = jnp.where(special & (zq >= 2) & jnp.logical_not(alone), 0.0, a)
        vb = jnp.where(zq >= 2, a, 0.0)
        if k0 == 0:
            vb = jnp.where(alone, jnp.where(ri == 0, roll(a, -4, 1), -roll(a, 4, 1)), vb)
        xh, xl = split(jnp.concatenate([va, vb], axis=0) if packed else a)
        o = dot3(xh, xl, fh(k0), fl(k0), NN)
        for half, pair in enumerate((first, second) if packed else (first,)):
            for ri_part in range(2):
                pair[ri_part].append(
                    [
                        o[32 * half + 8 * q : 32 * half + 8 * q + 8, 128 * ri_part : 128 * ri_part + 128]
                        for q in range(4)
                    ]
                )
    return first, second


def low_forward(r1):
    inner = [
        four_point([(r1(zh * 4 + zl, 0), r1(zh * 4 + zl, 1)) for zl in range(4)], -1)
        for zh in range(4)
    ]
    yr, yi = [], []
    for k0 in range(4):
        o = four_point([inner[zh][k0] for zh in range(4)], -1)
        yr.append([p[0] for p in o])
        yi.append([p[1] for p in o])
    return yr, yi


def low_backward(y):
    inner = [four_point(list(zip(y[0][k0], y[1][k0])), 1) for k0 in range(4)]
    return [four_point([inner[k0][zh] for k0 in range(4)], 1) for zh in range(4)]


def merge_planes(first, second, off):
    a = low_backward(first)
    if second is None:
        return [a[z // 4][z % 4] for z in range(16)]
    special = (iota((8, 128), 0) & 1) + off == 0
    b = low_backward(second)
    return [
        (a[z // 4][z % 4][0], jnp.where(special, b[z // 4][z % 4][0], a[z // 4][z % 4][1]))
        for z in range(16)
    ]


def twist(x, c, s):
    return x * c + sub4(x) * s


def x_input(r2, tc, ts):
    return jnp.concatenate([twist(r2(u), tc(u), ts(u)) for u in range(32)], axis=0)


def conjugate(v):
    lane, row = iota((8, 128), 1), iota((8, 128), 0)
    kx0 = (lane >> 3) & 3
    w = jnp.where(kx0 == 1, roll(v, -16, 1), jnp.where(kx0 == 3, roll(v, 16, 1), v))
    return jnp.where(row < 4, w, -w)


def coefficients(sm, sa, off, off_u):
    lane, row = iota((8, 128), 1), iota((8, 128), 0)
    zq = row & 3
    special = (lane >> 5) + (lane & 1) + (zq & 1) + off + off_u == 0
    c1 = jnp.where(special, 0.5 * SCALE * (sm + sa), 2.0 * SCALE * sm)
    half = 0.5 * SCALE * (sm - sa)
    c2 = jnp.where(special, jnp.where(zq < 2, half, -half), 0.0)
    return c1, c2


def spread_spectrum(rows, pick):
    lane = iota((8, 128), 1)
    keep = [(lane & 3) == kx0 for kx0 in range(4)]
    cols = []
    for zq in range(4):
        parts = []
        for alt in range(2):
            b = rows(zq, alt)
            for k0 in range(4):
                for kx0 in range(4):
                    parts.append(jnp.where(keep[kx0], b[8 * k0 : 8 * k0 + 8], 0.0))
        cols.append(jnp.concatenate(parts, axis=0))
    m = jnp.concatenate(cols, axis=1)
    h, l = split(m)
    return dot(pick, h, NT) + dot(pick, l, NT)


def z_backward_fold(o):
    lane = iota((8, 128), 1)
    e = [[[None] * 4 for _ in range(2)] for _ in range(4)]
    for tx in range(4):
        for a in range(2):
            for tz in range(4):
                acc = o(tx, 0, a, tz)
                for r8 in range(1, 8):
                    acc = jnp.where((lane >> 4) == r8, o(tx, r8, a, tz), acc)
                e[tx][a][tz] = acc
    return e


def far_of(proj, pot):
    out = []
    for p in range(8):
        acc = proj(p, 0) * pot[0]
        for v in range(1, 32):
            acc = acc + proj(p, v) * pot[v]
        out.append(acc)
    return out


def near_of(plane, above, below, codes, near):
    lane, row = iota((8, 128), 1), iota((8, 128), 0)
    l, zc = row & 3, lane & 15
    code = [codes(k) for k in range(6)]
    picked = [[jnp.zeros((8, 128), F32)] * 4 for _ in range(6)]
    for d in range(3):
        for i in range(4):
            v = plane(d, i)
            up = roll(v, -16, 1)
            nxt = jnp.where(l == 3, roll(below(d, i), -16, 1), roll(up, -1, 0))
            after = jnp.where(lane >= 112, nxt, up)
            dn = roll(v, 16, 1)
            prv = jnp.where(l == 0, roll(above(d, i), 16, 1), roll(dn, 1, 0))
            before = jnp.where(lane < 16, prv, dn)
            for e, w in enumerate((before, v, after)):
                plus = jnp.where(zc == 15, roll(w, 15, 1), roll(w, -1, 1))
                minus = jnp.where(zc == 0, roll(w, -15, 1), roll(w, 1, 1))
                for f, x in enumerate((minus, w, plus)):
                    for k in range(6):
                        if k == 0 and (d, e, f) != (1, 1, 1):
                            continue
                        if k > 0 and (d, e, f) == (1, 1, 1):
                            continue
                        picked[k][i] = (
                            x if k == 0 else jnp.where(code[k] == 9 * d + 3 * e + f, x, picked[k][i])
                        )
    out = []
    for p in range(8):
        acc = None
        for k in range(6):
            for i in range(4):
                t = near(k, p, i) * picked[k][i]
                acc = t if acc is None else acc + t
        out.append(acc)
    return out


def z_order():
    out = []
    for step in range(8, 0, -1):
        out += [step] if step == 8 else [step, 16 - step]
    return out


def u_order():
    far = (0, 1, 2, 1)
    out = [(x, y, c) for x in range(4) for y in range(4) for c in range(2)]
    out.remove((0, 0, 0))
    return sorted(out, key=lambda t: (-far[t[0]] - far[t[1]], t))


def body(
    ch,
    cnt,
    proj,
    near,
    nbr,
    spec,
    *rest,
):
    tab_in, (out,), scr = rest[:15], rest[15:16], rest[16:]
    tab = scr[:15]
    (ch_s, cnt_s, proj_s, near_s, nbr_s) = scr[15:20]
    (sp, bm, nd, tp_h, tp_l) = scr[20:25]
    (s1, r1, s2, r2, s3, r3, s4, r4) = scr[25:33]
    (ms, bf, bl, hp, ha, hb, cc, rb, rs) = scr[33:42]
    (k_main, k_conj, extra) = scr[42:45]
    (in_sem, tab_sem, loc_sem, snd, rcv, rsem) = scr[45:]
    (wzh, wzl, fh, fl, gh, gl, gth, gtl, t1c, t1s, t2c, t2s, pick, wxh, wxl) = tab

    slab, zl = lax.axis_index("slab"), lax.axis_index("cell")
    slabs = lax.axis_size("slab")
    zh, u = slab // NU, slab % NU
    z = zh * 4 + zl
    off = z
    off_u = u

    def z_dev(t):
        return ((t // 4) * NU + u, t % 4)

    def z_peer(d):
        t = (z + d + 16) % 16
        return t, z_dev(t)

    def u_peer(d):
        t = ((u // 8 + d[0]) % 4) * 8 + ((u // 2 % 4 + d[1]) % 4) * 2 + (u + d[2]) % 2
        return t, (zh * NU + t, zl)

    def near_peer(e, f):
        return ((slab + slabs + e) % slabs, (zl + 4 + f) % 4)

    halo = [(e, f) for e in (-1, 0, 1) for f in (-1, 0, 1) if (e, f) != (0, 0)]

    first = [
        pltpu.make_async_copy(a, b, in_sem.at[i])
        for i, (a, b) in enumerate(
            ((ch, ch_s), (cnt, cnt_s), (proj, proj_s), (nbr, nbr_s), (near, near_s))
        )
    ]
    load = [pltpu.make_async_copy(a, b, tab_sem.at[i]) for i, (a, b) in enumerate(zip(tab_in, tab))]
    for c in first[:3] + load[:2]:
        c.start()

    barrier = pltpu.get_barrier_semaphore()
    peers = [z_peer(d)[1] for d in (12, 4, 13, 3, 14, 2, 15, 1)] + [u_peer(d)[1] for d in u_order()]
    for p in peers:
        pl.semaphore_signal(barrier, inc=1, device_id=p, device_id_type=pl.DeviceIdType.MESH)
    for c in load[2:] + first[3:]:
        c.start()
    own = [
        pltpu.make_async_copy(spec.at[z + 16 * j], sp.at[zh, j], loc_sem.at[j]) for j in range(3)
    ]
    for c in own:
        c.start()

    def send(src, dst, i, dev, arrival=None):
        pltpu.make_async_remote_copy(
            src_ref=src,
            dst_ref=dst,
            send_sem=snd.at[i],
            recv_sem=rcv.at[i] if arrival is None else arrival,
            device_id=dev,
            device_id_type=pl.DeviceIdType.MESH,
        ).start()

    def done(sem, i, ref):
        pltpu.make_async_copy(ref, ref, sem.at[i]).wait()

    first[0].wait()
    first[1].wait()
    half = cnt_s[...]
    cc[0:4, :] = half
    cc[4:8, :] = half
    mv = masked_charges(lambda i: ch_s[8 * i : 8 * i + 8, :], cc[...])
    for i in range(4):
        ms[8 * i : 8 * i + 8, :] = mv[i]
        for h in range(2):
            bf[2 * i + h : 2 * i + h + 1, :] = mv[i][4 * h : 4 * h + 1]
            bl[2 * i + h : 2 * i + h + 1, :] = mv[i][4 * h + 3 : 4 * h + 4]
    m = both_halves(mv)
    first[2].wait()

    def proj_at(p, v):
        r = (p * 32 + v) * 8
        return proj_s[r : r + 8, :]

    base = regroup(tiles_of(proj_at, m))
    lane16 = iota((16, 128), 1)
    keep = [jnp.where((lane16 >> 4) == r8, 1.0, 0.0).astype(BF16) for r8 in range(8)]
    for tx in range(4):
        for tz in range(4):
            h, l = split(jnp.concatenate([base[tx][0][tz], base[tx][1][tz]], axis=0))
            for r8 in range(8):
                r = tx * 128 + r8 * 16
                tp_h[r : r + 16, tz * 128 : tz * 128 + 128] = h * keep[r8]
                tp_l[r : r + 16, tz * 128 : tz * 128 + 128] = l * keep[r8]
    load[0].wait()
    load[1].wait()
    o = dot3(wzh[...], wzl[...], tp_h[...], tp_l[...], NT)
    for t in range(16):
        for ri in range(2):
            for tx in range(4):
                r = t * 4 + ri * 2
                s1[t, ri, 2 * tx : 2 * tx + 2, :] = o[r : r + 2, tx * 128 : tx * 128 + 128]
    pl.semaphore_wait(barrier, len(peers))

    core = u % 2
    opp_in, opp_out = (z + 12 + 8 * core) % 16, (z + 4 + 8 * core) % 16
    relays = []
    for m in (3, 2, 1):
        for side, sgn in ((0, 1 - 2 * core), (1, 2 * core - 1)):
            relays.append((side * 3 + m - 1, (z + 16 + sgn * (4 + m)) % 16, z_peer(4 * sgn)[1], z_peer(-4 * sgn)[0], z_peer(m * sgn)[1]))
    opp = (6, (z + 8) % 16, z_dev(opp_out), opp_in, z_dev(opp_out))
    relays = [opp] + relays
    for slot, t, dev, _, _ in relays:
        send(s1.at[t], rb.at[slot], 0, dev, rsem.at[slot])
    for d in (4, 12, 3, 13, 2, 14, 1, 15):
        t, dev = z_peer(d + core * (16 - 2 * d))
        send(s1.at[t], r1.at[z], 0, dev)
    r1[pl.ds(z, 1)] = s1[pl.ds(z, 1)]

    far_id = (z + 8) % 16
    for j in range(2):
        send(spec.at[far_id + 16 * j], rs.at[j], 4, z_dev(opp_out), rsem.at[7 + j])

    @pl.when(far_id == 0)
    def _():
        send(spec.at[far_id + 32], rs.at[2], 5, z_dev(opp_out), rsem.at[9])

    for slot, _, _, src, dev in relays:
        done(rsem, slot, rb.at[slot])
        send(rb.at[slot], r1.at[src], 10, dev, rcv.at[0])

    for d in (4, 12):
        t, dev = z_peer(d)
        for j in range(2):
            send(spec.at[t + 16 * j], sp.at[zh, j], 4, dev)

        @pl.when(t == 0)
        def _():
            send(spec.at[t + 32], sp.at[zh, 2], 5, dev)

    for j in range(2):
        done(rsem, 7 + j, rs.at[j])
        send(rs.at[j], sp.at[opp_in // 4, j], 11, z_dev(opp_out), rcv.at[4])

    @pl.when(opp_out == 0)
    def _():
        done(rsem, 9, rs.at[2])
        send(rs.at[2], sp.at[opp_in // 4, 2], 12, z_dev(opp_out), rcv.at[5])

    for i in (2, 3):
        load[i].wait()
    done(rcv, 0, s1.at[pl.ds(0, 15)])

    zero = jnp.zeros((8, 128), F32)

    def y_stage(packed):
        whole = low_forward(lambda t, ri: r1[t, ri])
        part = low_forward(lambda t, ri: zero if ri else r1[t, 0]) if packed else None
        y = y_forward(whole, part, lambda k: fh[k], lambda k: fl[k], off)
        for t in range(32):
            s2[t] = y[8 * t : 8 * t + 8]

    pl.when(z == 0)(lambda: y_stage(True))
    pl.when(z != 0)(lambda: y_stage(False))
    for d in u_order():
        t, dev = u_peer(d)
        send(s2.at[t], r2.at[u], 1, dev)
    r2[pl.ds(u, 1)] = s2[pl.ds(u, 1)]

    for i in range(4, 15):
        load[i].wait()
    for c in own:
        c.wait()
    done(rcv, 4, sp.at[pl.ds(0, 3), pl.ds(0, 2)])

    @pl.when(z == 0)
    def _():
        done(rcv, 5, sp.at[pl.ds(0, 3), 0])

    packed = jnp.where(z == 0, 2, 0)
    for zq in range(4):
        for alt in range(2):
            src = (packed if (zq >= 2) != (alt == 1) else 0, 1)
            for k0 in range(4):
                for pos in range(4):
                    k2 = POS_OF_K2.index(pos)
                    for j in range(2):
                        r = k0 * 8 + pos * 2 + j
                        bm[zq, alt, r : r + 1, :] = sp[
                            zq, src[j], k0 : k0 + 1, k2 * 128 : k2 * 128 + 128
                        ]
    sm = spread_spectrum(lambda zq, alt: bm[zq, alt], pick[...])
    for k1 in range(32):
        a = slice(8 * k1, 8 * k1 + 8)
        c1, c2 = coefficients(sm[a, :128], sm[a, 128:], off, off_u)
        k_main[k1] = c1
        k_conj[k1] = c2
        extra[k1] = zero

    done(rcv, 1, s2.at[pl.ds(0, 31)])

    def rows8(ref):
        return lambda i: ref[8 * i : 8 * i + 8, :]

    def x_forward(r):
        xh, xl = split(x_input(r, rows8(t1c), rows8(t1s)))
        q = dot3(gh[...], gl[...], xh, xl, NN)
        out = []
        for k1 in range(32):
            a = slice(8 * k1, 8 * k1 + 8)
            out.append(lane_dft4(twist(q[a], t2c[a, :], t2s[a, :]), -1))
        return out

    @pl.when(z + u == 0)
    def _():
        for k1, b in enumerate(x_forward(lambda t: conjugate(r2[t]))):
            extra[k1] = b * k_conj[k1]

    ws = []
    for k1, b in enumerate(x_forward(lambda t: r2[t])):
        a = slice(8 * k1, 8 * k1 + 8)
        w = lane_dft4(b * k_main[k1] + extra[k1], 1)
        ws.append(twist(w, t2c[a, :], -t2s[a, :]))
    xh, xl = split(jnp.concatenate(ws, axis=0))
    o = dot3(gth[...], gtl[...], xh, xl, NN)
    for t in range(32):
        a = slice(8 * t, 8 * t + 8)
        s3[t] = twist(o[a], t1c[a, :], -t1s[a, :])
    for d in u_order():
        t, dev = u_peer(d)
        send(s3.at[t], r3.at[u], 2, dev)
    r3[pl.ds(u, 1)] = s3[pl.ds(u, 1)]

    for e, f in halo:
        dev = near_peer(e, f)
        if f == 0:
            send(ms, hp.at[(1 - e) // 2], 6 + (1 - e) // 2, dev)
        elif f == 1:
            send(bl, ha.at[1 - e], 8, dev)
        else:
            send(bf, hb.at[1 - e], 9, dev)
    done(rcv, 2, s3.at[pl.ds(0, 31)])


    def y_back_stage(packed):
        v = jnp.concatenate([r3[t] for t in range(32)], axis=0)
        a, b = y_backward(v, lambda k: fh[k], lambda k: fl[k], off, packed)
        blocks = merge_planes(a, b if packed else None, off)
        for t in range(16):
            for ri in range(2):
                s4[t, ri] = blocks[t][ri]

    pl.when(z == 0)(lambda: y_back_stage(True))
    pl.when(z != 0)(lambda: y_back_stage(False))
    for d in z_order():
        t, dev = z_peer(d + core * (16 - 2 * d))
        send(s4.at[t], r4.at[z], 3, dev)
    r4[pl.ds(z, 1)] = s4[pl.ds(z, 1)]

    first[3].wait()
    first[4].wait()
    for k in range(6):
        half = nbr_s[4 * k : 4 * k + 4, :]
        nd[k, 0:4, :] = half
        nd[k, 4:8, :] = half
    done(rcv, 6, hp.at[0])
    done(rcv, 7, hp.at[0])
    done(rcv, 8, ha)
    done(rcv, 9, hb)

    def plane(d, i):
        a = slice(8 * i, 8 * i + 8)
        return ms[a, :] if d == 1 else hp[d // 2, a, :]

    low = iota((8, 128), 0) < 4

    def edge(ref):
        def get(d, i):
            pair = ref[d, 2 * i : 2 * i + 2, :]
            return jnp.where(
                low,
                jnp.broadcast_to(pair[0:1], (8, 128)),
                jnp.broadcast_to(pair[1:2], (8, 128)),
            )

        return get

    def near_at(k, p, i):
        r = ((k * 8 + p) * 4 + i) * 8
        return near_s[r : r + 8, :]

    near_sum = near_of(plane, edge(ha), edge(hb), lambda k: nd[k], near_at)

    done(rcv, 3, s4.at[pl.ds(0, 15)])

    rt = jnp.concatenate([r4[t, ri] for t in range(16) for ri in range(2)], axis=0).T
    th, tl = split(rt)
    xs_h, xs_l = [], []
    for tx in range(4):
        mk = jnp.where(((lane16 >> 1) & 3) == tx, 1.0, 0.0).astype(BF16)
        mk = jnp.concatenate([jnp.concatenate([mk, mk], axis=1)] * 8, axis=0)
        xs_h.append(th * mk)
        xs_l.append(tl * mk)
    o = dot3(jnp.concatenate(xs_h, axis=0), jnp.concatenate(xs_l, axis=0), wxh[...], wxl[...], NN)

    def o_at(tx, r8, a, tz):
        r = tx * 128 + r8 * 16 + a * 8
        return o[r : r + 8, tz * 128 : tz * 128 + 128]

    far = far_of(proj_at, ungroup(z_backward_fold(o_at)))
    row = iota((8, 128), 0)
    both = cc[...]
    for i in range(4):
        a, b = far[2 * i] + near_sum[2 * i], far[2 * i + 1] + near_sum[2 * i + 1]
        tot = jnp.where(low, a + sub4(a), b + sub4(b))
        out[8 * i : 8 * i + 8, :] = jnp.where(2 * i + (row >> 2) < both, tot, 0.0)

    done(snd, 0, s1.at[pl.ds(0, 15)])
    done(snd, 1, s2.at[pl.ds(0, 31)])
    done(snd, 2, s3.at[pl.ds(0, 31)])
    done(snd, 3, s4.at[pl.ds(0, 15)])
    done(snd, 4, sp.at[pl.ds(0, 3), pl.ds(0, 2)])

    for t in ((z + 8) % 16, (z + 4) % 16, (z + 12) % 16):

        @pl.when(t == 0)
        def _():
            done(snd, 5, sp.at[0, 0])

    @pl.when(opp_out == 0)
    def _():
        done(snd, 12, sp.at[0, 0])

    done(snd, 10, s1.at[pl.ds(0, 7)])
    done(snd, 11, rs.at[pl.ds(0, 2)])

    done(snd, 6, ms)
    done(snd, 7, ms)
    done(snd, 8, ha)
    done(snd, 9, hb)


def per_device(charges, counts, projection, near_blocks, neighbours, spectrum):
    tabs = [jnp.asarray(t) for t in tables()]
    ins = [
        charges.reshape(32, 128),
        counts.reshape(4, 128),
        projection.reshape(2048, 128),
        near_blocks.reshape(1536, 128),
        neighbours.reshape(24, 128),
        jnp.transpose(spectrum, (1, 2, 0)),
    ]
    vm = pltpu.VMEM
    scratch = [vm(t.shape, t.dtype) for t in tabs]
    scratch += [vm(a.shape, a.dtype) for a in ins[:5]]
    scratch += [
        vm((4, 3, 4, 512), F32),
        vm((4, 2, 32, 128), F32),
        vm((6, 8, 128), jnp.int32),
        vm((512, 512), BF16),
        vm((512, 512), BF16),
    ]
    scratch += [vm((16, 2, 8, 128), F32)] * 2 + [vm((32, 8, 128), F32)] * 4
    scratch += [vm((16, 2, 8, 128), F32)] * 2
    scratch += [
        vm((32, 128), F32),
        vm((8, 128), F32),
        vm((8, 128), F32),
        vm((2, 32, 128), F32),
        vm((3, 8, 128), F32),
        vm((3, 8, 128), F32),
        vm((8, 128), jnp.int32),
        vm((7, 2, 8, 128), F32),
        vm((3, 4, 512), F32),
    ]
    scratch += [vm((32, 8, 128), F32)] * 3
    dma = pltpu.SemaphoreType.DMA
    scratch += [dma((5,)), dma((15,)), dma((3,)), dma((13,)), dma((10,)), dma((10,))]
    res = pl.pallas_call(
        body,
        out_shape=jax.ShapeDtypeStruct((32, 128), F32),
        in_specs=[pl.BlockSpec(memory_space=pl.ANY)] * (6 + len(tabs)),
        out_specs=pl.BlockSpec(memory_space=pltpu.VMEM),
        scratch_shapes=scratch,
        compiler_params=pltpu.CompilerParams(collective_id=0, has_side_effects=True),
        name="potential",
    )(*ins, *tabs)
    return res.reshape(8, 1, 512)


def solution(mesh):
    in_specs = (
        P(None, "slab", "cell"),
        P("slab", "cell"),
        P(None, None, "slab", "cell"),
        P(None, None, None, "slab", "cell"),
        P(None, "slab", "cell"),
        P(None, None, "slab"),
    )
    return jax.shard_map(
        per_device, mesh=mesh, in_specs=in_specs, out_specs=P(None, "slab", "cell"), check_vma=False
    )
```

```python
import functools

import jax
import jax.numpy as jnp
import numpy as np
from jax import lax
from jax.experimental import pallas as pl
from jax.experimental.pallas import tpu as pltpu
from jax.sharding import PartitionSpec as P

F32 = jnp.float32
BF16 = jnp.bfloat16
NZ_RING = 16
NU = 32
SCALE = 1.0 / 16777216.0
POS_OF_K2 = (0, 2, 1, 3)


def split_np(table):
    hi = table.astype(np.float32).astype(jnp.bfloat16)
    lo = (table - hi.astype(np.float64)).astype(jnp.bfloat16)
    return hi, lo


def cis(num, den):
    ang = 2.0 * np.pi * (num % den) / den
    return np.cos(ang), np.sin(ang)


def slot_freq(z, j):
    return z + 16 * j


def z_table():
    tab = np.zeros((16, 2, 2, 4, 8, 16))
    zc = np.arange(16)
    for z in range(16):
        for j in range(2):
            for tz in range(4):
                gz = zc * 4 + tz
                if z == 0 and j == 0:
                    re, im = np.ones(16), 1.0 - 2.0 * (gz % 2)
                else:
                    c, s = cis(slot_freq(z, j) * gz, 64)
                    re, im = c, -s
                tab[z, 0, j, tz] = re
                tab[z, 1, j, tz] = im
    return tab.reshape(64, 512)


def z_table_wide():
    tab = z_table().reshape(16, 2, 1, 2, 512)
    return np.broadcast_to(tab, (16, 2, 4, 2, 512)).reshape(256, 512)


def y_table():
    r8, ty, l = np.meshgrid(np.arange(8), np.arange(4), np.arange(4), indexing="ij")
    low = (l * 32 + r8 * 4 + ty).reshape(-1)
    k0, u, zq = np.meshgrid(np.arange(4), np.arange(32), np.arange(4), indexing="ij")
    ky = zq * 128 + u * 4 + k0
    c, s = cis(ky[..., None] * low, 512)
    tab = np.zeros((4, 32, 2, 4, 2, 128))
    tab[:, :, 0, :, 0] = c
    tab[:, :, 0, :, 1] = s
    tab[:, :, 1, :, 0] = -s
    tab[:, :, 1, :, 1] = c
    return tab.reshape(4, 256, 256)


def x_table():
    c, s = cis(np.arange(32)[:, None] * np.arange(32)[None, :], 32)
    tab = np.zeros((32, 2, 4, 32, 2, 4))
    for q in range(4):
        tab[:, 0, q, :, 0, q] = c
        tab[:, 0, q, :, 1, q] = s
        tab[:, 1, q, :, 0, q] = -s
        tab[:, 1, q, :, 1, q] = c
    return tab.reshape(256, 256)


def lane_parts():
    lane = np.arange(128)
    return lane // 32, (lane // 8) % 4, (lane // 2) % 4, lane % 2


def twist_table(u_or_k1, second):
    k0, kx0, tx, _ = lane_parts()
    row = np.arange(32)[:, None]
    num = tx[None] * (kx0[None] + 4 * row) if second else 4 * row * kx0[None]
    c, s = cis(num, 512)
    cc = np.zeros((32, 2, 4, 128))
    ss = np.zeros((32, 2, 4, 128))
    cc[:] = c[:, None, None, :]
    ss[:, 0] = s[:, None, :]
    ss[:, 1] = -s[:, None, :]
    return cc.reshape(256, 128).astype(np.float32), ss.reshape(256, 128).astype(np.float32)


def pick_table():
    tab = np.zeros((32, 2, 4, 4, 128))
    for k1 in range(32):
        for q in range(4):
            tab[k1, :, q, q, 4 * k1 : 4 * k1 + 4] = 1.0
    return tab.reshape(256, 512)


@functools.cache
def tables():
    out = []
    zt = z_table()
    out += list(split_np(zt))
    out += list(split_np(y_table()))
    g = x_table()
    out += list(split_np(g))
    out += list(split_np(g.T))
    out += list(twist_table(None, False))
    out += list(twist_table(None, True))
    out.append(pick_table().astype(jnp.bfloat16))
    out += list(split_np(z_table_wide()))
    return tuple(np.asarray(t) for t in out)


def roll(x, shift, axis):
    if axis == 1 and x.shape[1] > 128:
        return jnp.concatenate([roll(x[:, i : i + 128], shift, 1) for i in range(0, x.shape[1], 128)], axis=1)
    return pltpu.roll(x, shift % x.shape[axis], axis)


def sub4(x):
    return roll(x, 4, 0)


def iota(shape, dim):
    return lax.broadcasted_iota(jnp.int32, shape, dim)


def split(x):
    hi = x.astype(BF16)
    return hi, (x - hi.astype(F32)).astype(BF16)


NN = (((1,), (0,)), ((), ()))
NT = (((1,), (1,)), ((), ()))


def dot(a, b, dims):
    return lax.dot_general(a, b, dims, preferred_element_type=F32)


def dot3(ah, al, bh, bl, dims):
    return dot(ah, bh, dims) + (dot(al, bh, dims) + dot(ah, bl, dims))


def four_point(parts, sign):
    (ar, ai), (br, bi), (cr, ci), (dr, di) = parts
    pr, pi, mr, mi = ar + cr, ai + ci, ar - cr, ai - ci
    qr, qi, nr, ni = br + dr, bi + di, br - dr, bi - di
    if sign < 0:
        return [(pr + qr, pi + qi), (mr + ni, mi - nr), (pr - qr, pi - qi), (mr - ni, mi + nr)]
    return [(pr + qr, pi + qi), (mr - ni, mi + nr), (pr - qr, pi - qi), (mr + ni, mi - nr)]


def lane_partner(x, stride, bit):
    return jnp.where(bit == 0, roll(x, -stride, 1), roll(x, stride, 1))


def swap_signed(x, ri, sign):
    r = sub4(x)
    return jnp.where(ri == 0, -r, r) if sign > 0 else jnp.where(ri == 0, r, -r)


def lane_dft4(x, sign):
    lane = iota(x.shape, 1)
    ri = (iota(x.shape, 0) >> 2) & 1
    b1, b0 = (lane >> 2) & 1, (lane >> 1) & 1
    if sign < 0:
        a = lane_partner(x, 4, b1)
        x = jnp.where(b1 == 0, x + a, a - x)
        x = jnp.where((b1 == 1) & (b0 == 1), swap_signed(x, ri, -1), x)
        c = lane_partner(x, 2, b0)
        return jnp.where(b0 == 0, x + c, c - x)
    c = lane_partner(x, 2, b0)
    x = jnp.where(b0 == 0, x + c, c - x)
    x = jnp.where((b1 == 1) & (b0 == 1), swap_signed(x, ri, 1), x)
    a = lane_partner(x, 4, b1)
    return jnp.where(b1 == 0, x + a, a - x)


def masked_charges(ch, cnt):
    row = iota((8, 128), 0)
    return [jnp.where(2 * i + (row >> 2) < cnt, ch(i), 0.0) for i in range(4)]


def both_halves(mv):
    row = iota((8, 128), 0)
    out = []
    for v in mv:
        r = sub4(v)
        out += [jnp.where(row < 4, v, r), jnp.where(row < 4, r, v)]
    return out


def tiles_of(proj, m):
    out = []
    for v in range(32):
        acc = proj(0, v) * m[0]
        for p in range(1, 8):
            acc = acc + proj(p, v) * m[p]
        out.append(acc)
    return out


def regroup(tile):
    low = iota((8, 128), 0) < 4
    base = [[[None] * 4 for _ in range(2)] for _ in range(4)]
    for tx in range(4):
        for a in range(2):
            for h in range(2):
                v0, v1 = tile[tx * 8 + 4 * a + h], tile[tx * 8 + 4 * a + 2 + h]
                base[tx][a][2 * h] = jnp.where(low, v0, sub4(v1))
                base[tx][a][2 * h + 1] = jnp.where(low, sub4(v0), v1)
    return base


def ungroup(e):
    low = iota((8, 128), 0) < 4
    out = [None] * 32
    for tx in range(4):
        for a in range(2):
            for h in range(2):
                p, q = e[tx][a][2 * h], e[tx][a][2 * h + 1]
                out[tx * 8 + 4 * a + h] = jnp.where(low, p, sub4(q))
                out[tx * 8 + 4 * a + 2 + h] = jnp.where(low, sub4(p), q)
    return out


def y_fixup(whole, part, k0, off):
    lane, row = iota(whole.shape, 1), iota(whole.shape, 0)
    zq, ri, u = lane & 3, (lane >> 2) & 1, lane >> 3
    rest = whole - part
    swapped = jnp.where(ri == 0, roll(rest, -4, 1), -roll(rest, 4, 1))
    alone = (u == 0) & ((zq & 1) == 0) if k0 == 0 else (lane < 0)
    special = ((row & 1) + off == 0) & jnp.logical_not(alone)
    return jnp.where(special, jnp.where(zq < 2, part, swapped), whole)


def y_forward(whole, part, fh, fl, off):
    rows = []
    for k0 in range(4):
        pairs = (whole,) if part is None else (whole, part)
        x = [jnp.concatenate([jnp.concatenate(y[k0], axis=0) for y in pair], axis=1) for pair in pairs]
        xh, xl = split(jnp.concatenate(x, axis=0))
        o = dot3(xh, xl, fh(k0), fl(k0), NT)
        rows.append(o if part is None else y_fixup(o[:32], o[32:], k0, off))
    return jnp.concatenate(rows, axis=0).T


def y_backward(v, fh, fl, off, packed=True):
    vt = v.T
    first, second = ([], []), ([], [])
    for k0 in range(4):
        a = vt[k0 * 32 : k0 * 32 + 32]
        lane, row = iota(a.shape, 1), iota(a.shape, 0)
        zq, ri, u = lane & 3, (lane >> 2) & 1, lane >> 3
        special = (row & 1) + off == 0
        alone = (u == 0) & ((zq & 1) == 0) if k0 == 0 else (lane < 0)
        va = jnp.where(special & (zq >= 2) & jnp.logical_not(alone), 0.0, a)
        vb = jnp.where(zq >= 2, a, 0.0)
        if k0 == 0:
            vb = jnp.where(alone, jnp.where(ri == 0, roll(a, -4, 1), -roll(a, 4, 1)), vb)
        xh, xl = split(jnp.concatenate([va, vb], axis=0) if packed else a)
        o = dot3(xh, xl, fh(k0), fl(k0), NN)
        for half, pair in enumerate((first, second) if packed else (first,)):
            for ri_part in range(2):
                pair[ri_part].append(
                    [
                        o[32 * half + 8 * q : 32 * half + 8 * q + 8, 128 * ri_part : 128 * ri_part + 128]
                        for q in range(4)
                    ]
                )
    return first, second


def low_forward(r1):
    inner = [
        four_point([(r1(zh * 4 + zl, 0), r1(zh * 4 + zl, 1)) for zl in range(4)], -1)
        for zh in range(4)
    ]
    yr, yi = [], []
    for k0 in range(4):
        o = four_point([inner[zh][k0] for zh in range(4)], -1)
        yr.append([p[0] for p in o])
        yi.append([p[1] for p in o])
    return yr, yi


def low_backward(y):
    inner = [four_point(list(zip(y[0][k0], y[1][k0])), 1) for k0 in range(4)]
    return [four_point([inner[k0][zh] for k0 in range(4)], 1) for zh in range(4)]


def merge_planes(first, second, off):
    a = low_backward(first)
    if second is None:
        return [a[z // 4][z % 4] for z in range(16)]
    special = (iota((8, 128), 0) & 1) + off == 0
    b = low_backward(second)
    return [
        (a[z // 4][z % 4][0], jnp.where(special, b[z // 4][z % 4][0], a[z // 4][z % 4][1]))
        for z in range(16)
    ]


def twist(x, c, s):
    return x * c + sub4(x) * s


def x_input(r2, tc, ts):
    return jnp.concatenate([twist(r2(u), tc(u), ts(u)) for u in range(32)], axis=0)


def conjugate(v):
    lane, row = iota((8, 128), 1), iota((8, 128), 0)
    kx0 = (lane >> 3) & 3
    w = jnp.where(kx0 == 1, roll(v, -16, 1), jnp.where(kx0 == 3, roll(v, 16, 1), v))
    return jnp.where(row < 4, w, -w)


def coefficients(sm, sa, off, off_u):
    lane, row = iota((8, 128), 1), iota((8, 128), 0)
    zq = row & 3
    special = (lane >> 5) + (lane & 1) + (zq & 1) + off + off_u == 0
    c1 = jnp.where(special, 0.5 * SCALE * (sm + sa), 2.0 * SCALE * sm)
    half = 0.5 * SCALE * (sm - sa)
    c2 = jnp.where(special, jnp.where(zq < 2, half, -half), 0.0)
    return c1, c2


def spread_spectrum(rows, pick):
    lane = iota((8, 128), 1)
    keep = [(lane & 3) == kx0 for kx0 in range(4)]
    cols = []
    for zq in range(4):
        parts = []
        for alt in range(2):
            b = rows(zq, alt)
            for k0 in range(4):
                for kx0 in range(4):
                    parts.append(jnp.where(keep[kx0], b[8 * k0 : 8 * k0 + 8], 0.0))
        cols.append(jnp.concatenate(parts, axis=0))
    m = jnp.concatenate(cols, axis=1)
    h, l = split(m)
    return dot(pick, h, NT) + dot(pick, l, NT)


def z_backward_fold(o):
    lane = iota((8, 128), 1)
    e = [[[None] * 4 for _ in range(2)] for _ in range(4)]
    for tx in range(4):
        for a in range(2):
            for tz in range(4):
                acc = o(tx, 0, a, tz)
                for r8 in range(1, 8):
                    acc = jnp.where((lane >> 4) == r8, o(tx, r8, a, tz), acc)
                e[tx][a][tz] = acc
    return e


def far_of(proj, pot):
    out = []
    for p in range(8):
        acc = proj(p, 0) * pot[0]
        for v in range(1, 32):
            acc = acc + proj(p, v) * pot[v]
        out.append(acc)
    return out


def near_of(plane, above, below, codes, near):
    lane, row = iota((8, 128), 1), iota((8, 128), 0)
    l, zc = row & 3, lane & 15
    code = [codes(k) for k in range(6)]
    picked = [[jnp.zeros((8, 128), F32)] * 4 for _ in range(6)]
    for d in range(3):
        for i in range(4):
            v = plane(d, i)
            up = roll(v, -16, 1)
            nxt = jnp.where(l == 3, roll(below(d, i), -16, 1), roll(up, -1, 0))
            after = jnp.where(lane >= 112, nxt, up)
            dn = roll(v, 16, 1)
            prv = jnp.where(l == 0, roll(above(d, i), 16, 1), roll(dn, 1, 0))
            before = jnp.where(lane < 16, prv, dn)
            for e, w in enumerate((before, v, after)):
                plus = jnp.where(zc == 15, roll(w, 15, 1), roll(w, -1, 1))
                minus = jnp.where(zc == 0, roll(w, -15, 1), roll(w, 1, 1))
                for f, x in enumerate((minus, w, plus)):
                    for k in range(6):
                        if k == 0 and (d, e, f) != (1, 1, 1):
                            continue
                        if k > 0 and (d, e, f) == (1, 1, 1):
                            continue
                        picked[k][i] = (
                            x if k == 0 else jnp.where(code[k] == 9 * d + 3 * e + f, x, picked[k][i])
                        )
    out = []
    for p in range(8):
        acc = None
        for k in range(6):
            for i in range(4):
                t = near(k, p, i) * picked[k][i]
                acc = t if acc is None else acc + t
        out.append(acc)
    return out


def z_order():
    out = []
    for step in range(8, 0, -1):
        out += [step] if step == 8 else [step, 16 - step]
    return out


def u_order():
    far = (0, 1, 2, 1)
    out = [(x, y, c) for x in range(4) for y in range(4) for c in range(2)]
    out.remove((0, 0, 0))
    return sorted(out, key=lambda t: (-far[t[0]] - far[t[1]], t))


def body(
    ch,
    cnt,
    proj,
    near,
    nbr,
    spec,
    *rest,
):
    tab_in, (out,), scr = rest[:15], rest[15:16], rest[16:]
    tab = scr[:15]
    (ch_s, cnt_s, proj_s, near_s, nbr_s) = scr[15:20]
    (sp, bm, nd, tp_h, tp_l) = scr[20:25]
    (s1, r1, s2, r2, s3, r3, s4, r4) = scr[25:33]
    (ms, bf, bl, hp, ha, hb, cc, rb, rs) = scr[33:42]
    (k_main, k_conj, extra) = scr[42:45]
    (in_sem, tab_sem, loc_sem, snd, rcv, rsem) = scr[45:]
    (wzh, wzl, fh, fl, gh, gl, gth, gtl, t1c, t1s, t2c, t2s, pick, wxh, wxl) = tab

    slab, zl = lax.axis_index("slab"), lax.axis_index("cell")
    slabs = lax.axis_size("slab")
    zh, u = slab // NU, slab % NU
    z = zh * 4 + zl
    off = z
    off_u = u

    def z_dev(t):
        return ((t // 4) * NU + u, t % 4)

    def z_peer(d):
        t = (z + d + 16) % 16
        return t, z_dev(t)

    def u_peer(d):
        side = 1 + 2 * (u % 2)
        t = ((u // 8 + side * d[0]) % 4) * 8 + ((u // 2 % 4 + side * d[1]) % 4) * 2 + (u + d[2]) % 2
        return t, (zh * NU + t, zl)

    def near_peer(e, f):
        return ((slab + slabs + e) % slabs, (zl + 4 + f) % 4)

    halo = [(e, f) for e in (-1, 0, 1) for f in (-1, 0, 1) if (e, f) != (0, 0)]

    first = [
        pltpu.make_async_copy(a, b, in_sem.at[i])
        for i, (a, b) in enumerate(
            ((ch, ch_s), (cnt, cnt_s), (proj, proj_s), (nbr, nbr_s), (near, near_s))
        )
    ]
    load = [pltpu.make_async_copy(a, b, tab_sem.at[i]) for i, (a, b) in enumerate(zip(tab_in, tab))]
    for c in first[:3] + load[:2]:
        c.start()

    barrier = pltpu.get_barrier_semaphore()
    peers = [z_peer(d)[1] for d in (12, 4, 13, 3, 14, 2, 15, 1)] + [u_peer(d)[1] for d in u_order()]
    for p in peers:
        pl.semaphore_signal(barrier, inc=1, device_id=p, device_id_type=pl.DeviceIdType.MESH)
    for c in load[2:] + first[3:]:
        c.start()
    own = [
        pltpu.make_async_copy(spec.at[z + 16 * j], sp.at[zh, j], loc_sem.at[j]) for j in range(3)
    ]
    for c in own:
        c.start()

    def send(src, dst, i, dev, arrival=None):
        pltpu.make_async_remote_copy(
            src_ref=src,
            dst_ref=dst,
            send_sem=snd.at[i],
            recv_sem=rcv.at[i] if arrival is None else arrival,
            device_id=dev,
            device_id_type=pl.DeviceIdType.MESH,
        ).start()

    def done(sem, i, ref):
        pltpu.make_async_copy(ref, ref, sem.at[i]).wait()

    first[0].wait()
    first[1].wait()
    half = cnt_s[...]
    cc[0:4, :] = half
    cc[4:8, :] = half
    mv = masked_charges(lambda i: ch_s[8 * i : 8 * i + 8, :], cc[...])
    for i in range(4):
        ms[8 * i : 8 * i + 8, :] = mv[i]
        for h in range(2):
            bf[2 * i + h : 2 * i + h + 1, :] = mv[i][4 * h : 4 * h + 1]
            bl[2 * i + h : 2 * i + h + 1, :] = mv[i][4 * h + 3 : 4 * h + 4]
    m = both_halves(mv)
    first[2].wait()

    def proj_at(p, v):
        r = (p * 32 + v) * 8
        return proj_s[r : r + 8, :]

    base = regroup(tiles_of(proj_at, m))
    lane16 = iota((16, 128), 1)
    keep = [jnp.where((lane16 >> 4) == r8, 1.0, 0.0).astype(BF16) for r8 in range(8)]
    for tx in range(4):
        for tz in range(4):
            h, l = split(jnp.concatenate([base[tx][0][tz], base[tx][1][tz]], axis=0))
            for r8 in range(8):
                r = tx * 128 + r8 * 16
                tp_h[r : r + 16, tz * 128 : tz * 128 + 128] = h * keep[r8]
                tp_l[r : r + 16, tz * 128 : tz * 128 + 128] = l * keep[r8]
    load[0].wait()
    load[1].wait()
    o = dot3(wzh[...], wzl[...], tp_h[...], tp_l[...], NT)
    for t in range(16):
        for ri in range(2):
            for tx in range(4):
                r = t * 4 + ri * 2
                s1[t, ri, 2 * tx : 2 * tx + 2, :] = o[r : r + 2, tx * 128 : tx * 128 + 128]
    pl.semaphore_wait(barrier, len(peers))

    core = u % 2
    opp_in, opp_out = (z + 12 + 8 * core) % 16, (z + 4 + 8 * core) % 16
    relays = []
    for m in (3, 2, 1):
        for side, sgn in ((0, 1 - 2 * core), (1, 2 * core - 1)):
            relays.append((side * 3 + m - 1, (z + 16 + sgn * (4 + m)) % 16, z_peer(4 * sgn)[1], z_peer(-4 * sgn)[0], z_peer(m * sgn)[1]))
    opp = (6, (z + 8) % 16, z_dev(opp_out), opp_in, z_dev(opp_out))
    relays = [opp] + relays
    for slot, t, dev, _, _ in relays:
        send(s1.at[t], rb.at[slot], 0, dev, rsem.at[slot])
    for d in (4, 12, 3, 13, 2, 14, 1, 15):
        t, dev = z_peer(d + core * (16 - 2 * d))
        send(s1.at[t], r1.at[z], 0, dev)
    r1[pl.ds(z, 1)] = s1[pl.ds(z, 1)]

    far_id = (z + 8) % 16
    for j in range(2):
        send(spec.at[far_id + 16 * j], rs.at[j], 4, z_dev(opp_out), rsem.at[7 + j])

    @pl.when(far_id == 0)
    def _():
        send(spec.at[far_id + 32], rs.at[2], 5, z_dev(opp_out), rsem.at[9])

    for slot, _, _, src, dev in relays:
        done(rsem, slot, rb.at[slot])
        send(rb.at[slot], r1.at[src], 10, dev, rcv.at[0])

    for d in (4, 12):
        t, dev = z_peer(d)
        for j in range(2):
            send(spec.at[t + 16 * j], sp.at[zh, j], 4, dev)

        @pl.when(t == 0)
        def _():
            send(spec.at[t + 32], sp.at[zh, 2], 5, dev)

    for j in range(2):
        done(rsem, 7 + j, rs.at[j])
        send(rs.at[j], sp.at[opp_in // 4, j], 11, z_dev(opp_out), rcv.at[4])

    @pl.when(opp_out == 0)
    def _():
        done(rsem, 9, rs.at[2])
        send(rs.at[2], sp.at[opp_in // 4, 2], 12, z_dev(opp_out), rcv.at[5])

    for i in (2, 3):
        load[i].wait()
    done(rcv, 0, s1.at[pl.ds(0, 15)])

    zero = jnp.zeros((8, 128), F32)

    def y_stage(packed):
        whole = low_forward(lambda t, ri: r1[t, ri])
        part = low_forward(lambda t, ri: zero if ri else r1[t, 0]) if packed else None
        y = y_forward(whole, part, lambda k: fh[k], lambda k: fl[k], off)
        for t in range(32):
            s2[t] = y[8 * t : 8 * t + 8]

    pl.when(z == 0)(lambda: y_stage(True))
    pl.when(z != 0)(lambda: y_stage(False))
    for d in u_order():
        t, dev = u_peer(d)
        send(s2.at[t], r2.at[u], 1, dev)
    r2[pl.ds(u, 1)] = s2[pl.ds(u, 1)]

    for i in range(4, 15):
        load[i].wait()
    for c in own:
        c.wait()
    done(rcv, 4, sp.at[pl.ds(0, 3), pl.ds(0, 2)])

    @pl.when(z == 0)
    def _():
        done(rcv, 5, sp.at[pl.ds(0, 3), 0])

    packed = jnp.where(z == 0, 2, 0)
    for zq in range(4):
        for alt in range(2):
            src = (packed if (zq >= 2) != (alt == 1) else 0, 1)
            for k0 in range(4):
                for pos in range(4):
                    k2 = POS_OF_K2.index(pos)
                    for j in range(2):
                        r = k0 * 8 + pos * 2 + j
                        bm[zq, alt, r : r + 1, :] = sp[
                            zq, src[j], k0 : k0 + 1, k2 * 128 : k2 * 128 + 128
                        ]
    sm = spread_spectrum(lambda zq, alt: bm[zq, alt], pick[...])
    for k1 in range(32):
        a = slice(8 * k1, 8 * k1 + 8)
        c1, c2 = coefficients(sm[a, :128], sm[a, 128:], off, off_u)
        k_main[k1] = c1
        k_conj[k1] = c2
        extra[k1] = zero

    done(rcv, 1, s2.at[pl.ds(0, 31)])

    def rows8(ref):
        return lambda i: ref[8 * i : 8 * i + 8, :]

    def x_forward(r):
        xh, xl = split(x_input(r, rows8(t1c), rows8(t1s)))
        q = dot3(gh[...], gl[...], xh, xl, NN)
        out = []
        for k1 in range(32):
            a = slice(8 * k1, 8 * k1 + 8)
            out.append(lane_dft4(twist(q[a], t2c[a, :], t2s[a, :]), -1))
        return out

    @pl.when(z + u == 0)
    def _():
        for k1, b in enumerate(x_forward(lambda t: conjugate(r2[t]))):
            extra[k1] = b * k_conj[k1]

    ws = []
    for k1, b in enumerate(x_forward(lambda t: r2[t])):
        a = slice(8 * k1, 8 * k1 + 8)
        w = lane_dft4(b * k_main[k1] + extra[k1], 1)
        ws.append(twist(w, t2c[a, :], -t2s[a, :]))
    xh, xl = split(jnp.concatenate(ws, axis=0))
    o = dot3(gth[...], gtl[...], xh, xl, NN)
    for t in range(32):
        a = slice(8 * t, 8 * t + 8)
        s3[t] = twist(o[a], t1c[a, :], -t1s[a, :])
    for d in u_order():
        t, dev = u_peer(d)
        send(s3.at[t], r3.at[u], 2, dev)
    r3[pl.ds(u, 1)] = s3[pl.ds(u, 1)]

    for e, f in halo:
        dev = near_peer(e, f)
        if f == 0:
            send(ms, hp.at[(1 - e) // 2], 6 + (1 - e) // 2, dev)
        elif f == 1:
            send(bl, ha.at[1 - e], 8, dev)
        else:
            send(bf, hb.at[1 - e], 9, dev)
    done(rcv, 2, s3.at[pl.ds(0, 31)])


    def y_back_stage(packed):
        v = jnp.concatenate([r3[t] for t in range(32)], axis=0)
        a, b = y_backward(v, lambda k: fh[k], lambda k: fl[k], off, packed)
        blocks = merge_planes(a, b if packed else None, off)
        for t in range(16):
            for ri in range(2):
                s4[t, ri] = blocks[t][ri]

    pl.when(z == 0)(lambda: y_back_stage(True))
    pl.when(z != 0)(lambda: y_back_stage(False))
    for d in z_order():
        t, dev = z_peer(d + core * (16 - 2 * d))
        send(s4.at[t], r4.at[z], 3, dev)
    r4[pl.ds(z, 1)] = s4[pl.ds(z, 1)]

    first[3].wait()
    first[4].wait()
    for k in range(6):
        half = nbr_s[4 * k : 4 * k + 4, :]
        nd[k, 0:4, :] = half
        nd[k, 4:8, :] = half
    done(rcv, 6, hp.at[0])
    done(rcv, 7, hp.at[0])
    done(rcv, 8, ha)
    done(rcv, 9, hb)

    def plane(d, i):
        a = slice(8 * i, 8 * i + 8)
        return ms[a, :] if d == 1 else hp[d // 2, a, :]

    low = iota((8, 128), 0) < 4

    def edge(ref):
        def get(d, i):
            pair = ref[d, 2 * i : 2 * i + 2, :]
            return jnp.where(
                low,
                jnp.broadcast_to(pair[0:1], (8, 128)),
                jnp.broadcast_to(pair[1:2], (8, 128)),
            )

        return get

    def near_at(k, p, i):
        r = ((k * 8 + p) * 4 + i) * 8
        return near_s[r : r + 8, :]

    near_sum = near_of(plane, edge(ha), edge(hb), lambda k: nd[k], near_at)

    done(rcv, 3, s4.at[pl.ds(0, 15)])

    rt = jnp.concatenate([r4[t, ri] for t in range(16) for ri in range(2)], axis=0).T
    th, tl = split(rt)
    xs_h, xs_l = [], []
    for tx in range(4):
        mk = jnp.where(((lane16 >> 1) & 3) == tx, 1.0, 0.0).astype(BF16)
        mk = jnp.concatenate([jnp.concatenate([mk, mk], axis=1)] * 8, axis=0)
        xs_h.append(th * mk)
        xs_l.append(tl * mk)
    o = dot3(jnp.concatenate(xs_h, axis=0), jnp.concatenate(xs_l, axis=0), wxh[...], wxl[...], NN)

    def o_at(tx, r8, a, tz):
        r = tx * 128 + r8 * 16 + a * 8
        return o[r : r + 8, tz * 128 : tz * 128 + 128]

    far = far_of(proj_at, ungroup(z_backward_fold(o_at)))
    row = iota((8, 128), 0)
    both = cc[...]
    for i in range(4):
        a, b = far[2 * i] + near_sum[2 * i], far[2 * i + 1] + near_sum[2 * i + 1]
        tot = jnp.where(low, a + sub4(a), b + sub4(b))
        out[8 * i : 8 * i + 8, :] = jnp.where(2 * i + (row >> 2) < both, tot, 0.0)

    done(snd, 0, s1.at[pl.ds(0, 15)])
    done(snd, 1, s2.at[pl.ds(0, 31)])
    done(snd, 2, s3.at[pl.ds(0, 31)])
    done(snd, 3, s4.at[pl.ds(0, 15)])
    done(snd, 4, sp.at[pl.ds(0, 3), pl.ds(0, 2)])

    for t in ((z + 8) % 16, (z + 4) % 16, (z + 12) % 16):

        @pl.when(t == 0)
        def _():
            done(snd, 5, sp.at[0, 0])

    @pl.when(opp_out == 0)
    def _():
        done(snd, 12, sp.at[0, 0])

    done(snd, 10, s1.at[pl.ds(0, 7)])
    done(snd, 11, rs.at[pl.ds(0, 2)])

    done(snd, 6, ms)
    done(snd, 7, ms)
    done(snd, 8, ha)
    done(snd, 9, hb)


def per_device(charges, counts, projection, near_blocks, neighbours, spectrum):
    tabs = [jnp.asarray(t) for t in tables()]
    ins = [
        charges.reshape(32, 128),
        counts.reshape(4, 128),
        projection.reshape(2048, 128),
        near_blocks.reshape(1536, 128),
        neighbours.reshape(24, 128),
        jnp.transpose(spectrum, (1, 2, 0)),
    ]
    vm = pltpu.VMEM
    scratch = [vm(t.shape, t.dtype) for t in tabs]
    scratch += [vm(a.shape, a.dtype) for a in ins[:5]]
    scratch += [
        vm((4, 3, 4, 512), F32),
        vm((4, 2, 32, 128), F32),
        vm((6, 8, 128), jnp.int32),
        vm((512, 512), BF16),
        vm((512, 512), BF16),
    ]
    scratch += [vm((16, 2, 8, 128), F32)] * 2 + [vm((32, 8, 128), F32)] * 4
    scratch += [vm((16, 2, 8, 128), F32)] * 2
    scratch += [
        vm((32, 128), F32),
        vm((8, 128), F32),
        vm((8, 128), F32),
        vm((2, 32, 128), F32),
        vm((3, 8, 128), F32),
        vm((3, 8, 128), F32),
        vm((8, 128), jnp.int32),
        vm((7, 2, 8, 128), F32),
        vm((3, 4, 512), F32),
    ]
    scratch += [vm((32, 8, 128), F32)] * 3
    dma = pltpu.SemaphoreType.DMA
    scratch += [dma((5,)), dma((15,)), dma((3,)), dma((13,)), dma((10,)), dma((10,))]
    res = pl.pallas_call(
        body,
        out_shape=jax.ShapeDtypeStruct((32, 128), F32),
        in_specs=[pl.BlockSpec(memory_space=pl.ANY)] * (6 + len(tabs)),
        out_specs=pl.BlockSpec(memory_space=pltpu.VMEM),
        scratch_shapes=scratch,
        compiler_params=pltpu.CompilerParams(collective_id=0, has_side_effects=True),
        name="potential",
    )(*ins, *tabs)
    return res.reshape(8, 1, 512)


def solution(mesh):
    in_specs = (
        P(None, "slab", "cell"),
        P("slab", "cell"),
        P(None, None, "slab", "cell"),
        P(None, None, None, "slab", "cell"),
        P(None, "slab", "cell"),
        P(None, None, "slab"),
    )
    return jax.shard_map(
        per_device, mesh=mesh, in_specs=in_specs, out_specs=P(None, "slab", "cell"), check_vma=False
    )
```
